32 devices in a mesh: fsdp: 8 (over z, y), dp: 4 (over x, core).
Axes of the slice: x: 2, y: 2, z: 4, core: 2. Of those that a mesh axis runs over, the one named last changes fastest.
Arguments:
- tokens: bfloat16 [32768, 960], P(('fsdp', 'dp')), may hold values from -6 to 6
- seq_lengths: int32 [32, 8], P(('fsdp', 'dp')), may hold values from 0 to 1024, as said below
- norm1_gain: bfloat16 [960], P('fsdp'), may hold values from 0.5 to 1.5
- q_weight: bfloat16 [960, 960], P('fsdp', 'dp'), may hold values from -0.1875 to 0.1875
- k_weight: bfloat16 [960, 320], P('fsdp', 'dp'), may hold values from -0.1875 to 0.1875
- v_weight: bfloat16 [960, 320], P('fsdp', 'dp'), may hold values from -0.1875 to 0.1875
- o_weight: bfloat16 [960, 960], P('fsdp', 'dp'), may hold values from -0.75 to 0.75
- norm2_gain: bfloat16 [960], P('fsdp'), may hold values from 0.5 to 1.5
- gate_weight: bfloat16 [960, 2560], P('fsdp', 'dp'), may hold values from -0.1875 to 0.1875
- up_weight: bfloat16 [960, 2560], P('fsdp', 'dp'), may hold values from -0.1875 to 0.1875
- down_weight: bfloat16 [2560, 960], P('fsdp', 'dp'), may hold values from -0.125 to 0.125
- cotangent: bfloat16 [32768, 960], P(('fsdp', 'dp')), may hold values from -6 to 6
Outputs:
- mixed: bfloat16 [32768, 960], P(('fsdp', 'dp'))
- grad_tokens: float32 [32768, 960], P(('fsdp', 'dp'))
- grad_norm1: float32 [960], P('fsdp')
- grad_q: float32 [960, 960], P('fsdp', 'dp')
- grad_k: float32 [960, 320], P('fsdp', 'dp')
- grad_v: float32 [960, 320], P('fsdp', 'dp')
- grad_o: float32 [960, 960], P('fsdp', 'dp')
- grad_norm2: float32 [960], P('fsdp')
- grad_gate: float32 [960, 2560], P('fsdp', 'dp')
- grad_up: float32 [960, 2560], P('fsdp', 'dp')
- grad_down: float32 [2560, 960], P('fsdp', 'dp')
The draws below stay inside these ranges and needn't reach their ends.
Inputs may be any that keep to these rules, and one draw needn't show every extreme that they name: `seq_lengths`: row d lists the lengths of the sequences packed one after another from the first of device d's 1024 slots; a length may be 0; a row sums to at most 1024, the rest of the slots being padding; in every draw some device holds a single sequence of exactly 1024 tokens.
All inputs are finite; a program needn't handle non-finite values.
Results may differ from the reference program's by a relative error of at most 0.017.
Values may be sent and summed in bfloat16 or wider, within the bound.
No kernel may reach another device: no remote copies, remote signals or barrier semaphores. Data moves between devices by JAX's collectives and lax.ppermute only.
A program may use at most 256 MiB of HBM per device.

```python
import math
import jax
import jax.numpy as jnp
from jax import lax

D = 960
QUERY_HEADS = 15
KEY_VALUE_HEADS = 5
HEAD_SIZE = 64
FF = 2560
TOK_DEV = 1024
SLOTS = 8
QW = 960
KW = 320
NDEV = 32
TOKENS = 32768


def draw_seq_lengths(key, part):
    subkeys = jax.random.split(jax.random.fold_in(key, 17), 4)
    full_device = jax.random.randint(subkeys[0], (), 0, NDEV)
    live_totals = jax.random.randint(subkeys[1], (NDEV,), TOK_DEV // 4, TOK_DEV + 1)
    seq_counts = jax.random.randint(subkeys[2], (NDEV,), 1, SLOTS + 1)
    devices = jnp.arange(NDEV)
    chosen = devices == full_device
    live_totals = jnp.where(chosen, TOK_DEV, live_totals).astype(jnp.int32)
    seq_counts = jnp.where(chosen, 1, seq_counts).astype(jnp.int32)
    cut_points = jax.random.randint(subkeys[3], (NDEV, SLOTS - 1), 0, TOK_DEV + 1)
    cut_points = cut_points % (live_totals[:, None] + 1)
    places = jnp.arange(SLOTS - 1)
    cut_points = jnp.where(places[None, :] < seq_counts[:, None] - 1, cut_points, live_totals[:, None])
    cut_points = jnp.sort(cut_points.astype(jnp.int32), axis=1)
    bounds = jnp.concatenate([jnp.zeros((NDEV, 1), jnp.int32), cut_points, live_totals[:, None]], axis=1)
    return (bounds[:, 1:] - bounds[:, :-1]).astype(jnp.int32)


def strengthened(array, key, source, target, parts, factor):
    owner, partner = [(jnp.arange(array.shape[axis_at]) // (array.shape[axis_at] // parts)).reshape([-1 if axis == axis_at else 1 for axis in range(array.ndim)]) for axis_at in (source, target)]
    chosen = jax.random.permutation(key, parts)[partner]
    strong = (owner == chosen) | (owner == (partner + parts // 2) % parts)
    return jnp.where(strong, factor * array, array)


def steps_of(own_key, dims, cuts, smallest, largest):
    level = 1.0
    for axis_at, parts in cuts:
        steps = jax.random.uniform(jax.random.fold_in(jax.random.fold_in(own_key, 6), axis_at), (parts,), jnp.float32, smallest / len(cuts), largest / len(cuts))
        level = level * jnp.repeat(jnp.exp(steps), dims[axis_at] // parts).reshape((-1,) + (1,) * (len(dims) - 1 - axis_at))
    return level


def centred(key, extent, deviation, most, cuts=(), held_as=jnp.bfloat16):
    gain = steps_of(key, extent, cuts, -0.22, 0.18) if cuts else 1.0
    entries = jax.random.normal(key, extent, jnp.float32) * deviation * gain
    return jnp.minimum(jnp.maximum(entries, -most), most).astype(held_as)


def bell_draw_with(key, shape, spread, limit, cuts, heavy, kind=jnp.bfloat16):
    array = spread * jax.random.normal(key, shape, jnp.float32)
    if cuts:
        array = array * steps_of(key, shape, cuts, -0.22, 0.18)
    return jnp.clip(strengthened(array, jax.random.fold_in(key, 3), *heavy), -limit, limit).astype(kind)


def setup_inputs(seed: int = 0) -> dict:
    streams_of = jax.random.split(jax.random.key(seed), 13)
    return {
        "tokens": centred(streams_of[0], (TOKENS, D), 1.0, 6.0, ((0, 32),)),
        "seq_lengths": draw_seq_lengths(jax.random.fold_in(streams_of[12], 71), 0),
        "norm1_gain": jnp.clip(1.0 + 0.1 * jax.random.normal(streams_of[2], (D,), jnp.float32), 0.5, 1.5).astype(jnp.bfloat16),
        "q_weight": centred(streams_of[3], (D, QW), D ** -0.5, 0.1875, ((0, 8), (1, 4))),
        "k_weight": centred(streams_of[4], (D, KW), D ** -0.5, 0.1875, ((0, 8), (1, 4))),
        "v_weight": centred(streams_of[5], (D, KW), D ** -0.5, 0.1875, ((0, 8), (1, 4))),
        "o_weight": centred(streams_of[6], (QW, D), (QW // 16) ** -0.5, 0.75, ((0, 8), (1, 4))),
        "norm2_gain": jnp.clip(1.0 + 0.1 * jax.random.normal(streams_of[7], (D,), jnp.float32), 0.5, 1.5).astype(jnp.bfloat16),
        "gate_weight": centred(streams_of[8], (D, FF), D ** -0.5, 0.1875, ((0, 8), (1, 4))),
        "up_weight": centred(streams_of[9], (D, FF), D ** -0.5, 0.1875, ((0, 8), (1, 4))),
        "down_weight": centred(streams_of[10], (FF, D), FF ** -0.5, 0.125, ((0, 8), (1, 4))),
        "cotangent": bell_draw_with(streams_of[11], (TOKENS, D), 1.0, 6.0, ((0, 32),), (0, 1, 32, 2.75)),
    }


@jax.custom_vjp
def reduced_precision(v):
    return lax.optimization_barrier(v.astype(jnp.bfloat16)).astype(jnp.float32)

@jax.custom_vjp
def low_back(v):
    return v

def low_keep(v):
    return (reduced_precision(v), None)

def low_pass(kept, grad):
    return (grad,)

def back_keep(v):
    return (v, None)

def back_low(kept, grad):
    return (reduced_precision(grad),)
reduced_precision.defvjp(low_keep, low_pass)
low_back.defvjp(back_keep, back_low)
epsilon = 1e-05
rope_base = 100000.0
masked_fill = -1e+30
highest = lax.Precision.HIGHEST

def layout(lengths_row):
    ends = jnp.cumsum(lengths_row).astype(jnp.int32)
    places = jnp.arange(TOK_DEV, dtype=jnp.int32)
    passed = (places[:, None] >= ends[None, :]).astype(jnp.int32)
    segment = lax.optimization_barrier(jnp.sum(passed, axis=1)).astype(jnp.int32)
    starts = lax.optimization_barrier(jnp.sum(passed * lengths_row[None, :], axis=1)).astype(jnp.int32)
    position = (places - starts).astype(jnp.int32)
    live_rows = (places < ends[SLOTS - 1]).astype(jnp.float32)
    return (segment, position, live_rows)

def rope_tables(position):
    halfway = HEAD_SIZE // 2
    exponent = jnp.arange(halfway, dtype=jnp.float32) * (2.0 / HEAD_SIZE)
    inverse = jnp.exp(-math.log(rope_base) * exponent)
    angle = position.astype(jnp.float32)[:, None] * inverse[None, :]
    return (jnp.cos(angle), jnp.sin(angle))

def apply_rotary(values, cosine_table, sine_table):
    halfway = HEAD_SIZE // 2
    first_half = values[..., :halfway]
    second_half = values[..., halfway:]
    cos_wide = cosine_table[:, None, :]
    sin_wide = sine_table[:, None, :]
    return jnp.concatenate([first_half * cos_wide - second_half * sin_wide, second_half * cos_wide + first_half * sin_wide], axis=-1)

def device_forward(tokens_wide, gain_one, query_w, key_w, value_w, output_w, gain_two, gate_w, up_w, down_w, segment, cosine_table, sine_table, live_rows):
    row_count = tokens_wide.shape[0]
    heads_per_group = QUERY_HEADS // KEY_VALUE_HEADS
    scale_one = lax.rsqrt(lax.optimization_barrier(jnp.mean(tokens_wide * tokens_wide, axis=1, keepdims=True)) + epsilon)
    normed_one = reduced_precision(tokens_wide * scale_one * gain_one[None, :])
    query_proj = low_back(jnp.dot(normed_one, query_w, precision=highest))
    key_projection = low_back(jnp.dot(normed_one, key_w, precision=highest))
    value_projection = reduced_precision(low_back(jnp.dot(normed_one, value_w, precision=highest)))
    rotated_query = reduced_precision(apply_rotary(query_proj.reshape(row_count, QUERY_HEADS, HEAD_SIZE), cosine_table, sine_table))
    rotated_key = reduced_precision(apply_rotary(key_projection.reshape(row_count, KEY_VALUE_HEADS, HEAD_SIZE), cosine_table, sine_table))
    grouped_queries = rotated_query.reshape(row_count, KEY_VALUE_HEADS, heads_per_group, HEAD_SIZE)
    value_row_slice = value_projection.reshape(row_count, KEY_VALUE_HEADS, HEAD_SIZE)
    raw_scores = jnp.einsum('tngd,und->ngtu', grouped_queries, rotated_key, precision=highest) * (1.0 / math.sqrt(HEAD_SIZE))
    places = jnp.arange(row_count)
    allowed = (segment[:, None] == segment[None, :]) & (places[None, :] <= places[:, None])
    scores = jnp.where(allowed[None, None], low_back(raw_scores), masked_fill)
    peak_score = lax.optimization_barrier(jnp.max(scores, axis=-1, keepdims=True))
    exp_scores = jnp.exp(scores - peak_score)
    attn_probs = exp_scores / lax.optimization_barrier(jnp.sum(exp_scores, axis=-1, keepdims=True))
    probs_low = reduced_precision(attn_probs)
    attended = jnp.einsum('ngtu,und->tngd', probs_low, value_row_slice, precision=highest).reshape(row_count, QUERY_HEADS * HEAD_SIZE)
    attended = reduced_precision(low_back(attended))
    branch_one = low_back(jnp.dot(attended, output_w, precision=highest))
    hidden_mid = tokens_wide + branch_one
    scale_two = lax.rsqrt(lax.optimization_barrier(jnp.mean(hidden_mid * hidden_mid, axis=1, keepdims=True)) + epsilon)
    normed_two = reduced_precision(hidden_mid * scale_two * gain_two[None, :])
    gate_proj = low_back(jnp.dot(normed_two, gate_w, precision=highest))
    up_proj = low_back(jnp.dot(normed_two, up_w, precision=highest))
    hidden_ff = reduced_precision(gate_proj * jax.nn.sigmoid(gate_proj) * up_proj)
    branch_two = low_back(jnp.dot(hidden_ff, down_w, precision=highest))
    return live_rows[:, None] * (hidden_mid + branch_two)

def reference(tokens, seq_lengths, norm1_gain, q_weight, k_weight, v_weight, o_weight, norm2_gain, gate_weight, up_weight, down_weight, cotangent):
    weights = (norm1_gain.astype(jnp.float32), q_weight.astype(jnp.float32), k_weight.astype(jnp.float32), v_weight.astype(jnp.float32), o_weight.astype(jnp.float32), norm2_gain.astype(jnp.float32), gate_weight.astype(jnp.float32), up_weight.astype(jnp.float32), down_weight.astype(jnp.float32))
    token_blocks = tokens.astype(jnp.float32).reshape(NDEV, TOK_DEV, D)
    cotangent_blocks = cotangent.astype(jnp.float32).reshape(NDEV, TOK_DEV, D)

    def one_device(carried, inputs):
        tokens_wide, upstream, lengths_row = inputs
        segment, position, live_rows = layout(lengths_row)
        cosine_table, sine_table = rope_tables(position)

        def forward(tokens_in, *params):
            return device_forward(tokens_in, *params, segment, cosine_table, sine_table, live_rows)
        outputs, pullback = jax.vjp(forward, tokens_wide, *weights)
        grads = pullback(upstream)
        carried = tuple((total + part_grad for total, part_grad in zip(carried, grads[1:])))
        return (carried, (outputs.astype(jnp.bfloat16), grads[0]))
    zero_filled = tuple((jnp.zeros_like(weight) for weight in weights))
    totals, (outputs, input_grads) = lax.scan(one_device, zero_filled, (token_blocks, cotangent_blocks, seq_lengths))
    return (outputs.reshape(TOKENS, D), input_grads.reshape(TOKENS, D), totals[0], totals[1], totals[2], totals[3], totals[4], totals[5], totals[6], totals[7], totals[8])
```

```python
import math

import jax
import jax.numpy as jnp
from jax import lax
from jax.sharding import PartitionSpec as P

QUERY_HEADS = 15
KEY_VALUE_HEADS = 5
HEAD_SIZE = 64
QUERY_BLOCK_ROWS = 512


epsilon = 1e-05
rope_base = 100000.0
masked_fill = -1e30


def layout(lengths_row, n_slots):
    slots = jnp.arange(lengths_row.shape[0])
    ends = jnp.sum(jnp.where(slots[None, :] <= slots[:, None], lengths_row[None, :], 0), axis=1)
    places = jnp.arange(n_slots, dtype=jnp.int32)
    passed = (places[:, None] >= ends[None, :]).astype(jnp.int32)
    segment = jnp.sum(passed, axis=1)
    starts = jnp.sum(passed * lengths_row[None, :], axis=1)
    live_total = ends[-1]
    return (segment, places - starts, (places < live_total).astype(jnp.float32), live_total)


def rope_tables(position):
    halfway = HEAD_SIZE // 2
    exponent = jnp.arange(halfway, dtype=jnp.float32) * (2.0 / HEAD_SIZE)
    inverse = jnp.exp(-math.log(rope_base) * exponent)
    angle = position.astype(jnp.float32)[:, None] * inverse[None, :]
    return (jnp.cos(angle), jnp.sin(angle))


def apply_rotary(values, cosine_table, sine_table):
    halfway = HEAD_SIZE // 2
    first_half = values[..., :halfway]
    second_half = values[..., halfway:]
    cos_wide = cosine_table[:, None, :]
    sin_wide = sine_table[:, None, :]
    return jnp.concatenate(
        [
            first_half * cos_wide - second_half * sin_wide,
            second_half * cos_wide + first_half * sin_wide,
        ],
        axis=-1,
    )


def inverse_rotary(grads, cosine_table, sine_table):
    halfway = HEAD_SIZE // 2
    first_half = grads[..., :halfway]
    second_half = grads[..., halfway:]
    cos_wide = cosine_table[:, None, :]
    sin_wide = sine_table[:, None, :]
    return jnp.concatenate(
        [
            first_half * cos_wide + second_half * sin_wide,
            second_half * cos_wide - first_half * sin_wide,
        ],
        axis=-1,
    )


def norm_scale(values):
    return lax.rsqrt(jnp.mean(values * values, axis=1, keepdims=True) + epsilon)


def norm_back(values, scale_rows, gain_wide, upstream):
    weighted = gain_wide[None, :] * upstream
    return scale_rows * weighted - values * scale_rows**3 * jnp.mean(
        weighted * values, axis=1, keepdims=True
    )


def block_scores(query_block_rows, key_rows, seg_query, seg_keys, starting_row, score_scale):
    scores = (
        jnp.einsum("tngd,und->ngtu", query_block_rows, key_rows, preferred_element_type=jnp.float32)
        * score_scale
    )
    query_place = starting_row + jnp.arange(query_block_rows.shape[0])
    key_place = jnp.arange(key_rows.shape[0])
    allowed = (seg_query[:, None] == seg_keys[None, :]) & (
        key_place[None, :] <= query_place[:, None]
    )
    return jnp.where(allowed[None, None], scores, masked_fill)


def shards(
    tokens,
    seq_lengths,
    norm1_gain,
    q_weight,
    k_weight,
    v_weight,
    o_weight,
    norm2_gain,
    gate_weight,
    up_weight,
    down_weight,
    cotangent,
):
    row_count = tokens.shape[0]
    dp_count = lax.axis_size("dp")
    fsdp_count = lax.axis_size("fsdp")
    heads_per_group = QUERY_HEADS // KEY_VALUE_HEADS
    score_scale = 1.0 / math.sqrt(HEAD_SIZE)
    n_blocks = row_count // QUERY_BLOCK_ROWS
    segment, position, live_rows, live_total = layout(seq_lengths[0], row_count)
    cosine_table, sine_table = rope_tables(position)
    both = ("fsdp", "dp")
    q_rows, q_cols = q_weight.shape
    k_cols = k_weight.shape[1]
    gains_local = jnp.stack([norm1_gain, norm2_gain], axis=1)
    pack_qkv = jnp.concatenate([q_weight, k_weight, v_weight, gains_local], axis=1)
    pack_od = jnp.concatenate([o_weight, down_weight], axis=0)
    pack_gu = jnp.concatenate([gate_weight, up_weight], axis=1)

    def gather(pack):
        whole = lax.all_gather(pack, both, axis=0, tiled=False)
        return whole.reshape((fsdp_count, dp_count) + pack.shape)

    def whole_of(pieces):
        f, d, r, c = pieces.shape
        return pieces.transpose(0, 2, 1, 3).reshape(f * r, d * c)

    def chunks_of(whole):
        r, c = whole.shape
        return whole.reshape(fsdp_count, r // fsdp_count, dp_count, c // dp_count).transpose(
            0, 2, 1, 3
        )

    def scatter(chunks):
        f, d, r, c = chunks.shape
        flat = chunks.astype(jnp.bfloat16).reshape(f * d, r, c)
        return lax.psum_scatter(flat, both, scatter_dimension=0, tiled=False).astype(jnp.float32)

    got_qkv = gather(pack_qkv)
    query_full = whole_of(got_qkv[..., :q_cols])
    key_full = whole_of(got_qkv[..., q_cols : q_cols + k_cols])
    value_full = whole_of(got_qkv[..., q_cols + k_cols : q_cols + 2 * k_cols])
    gain_one = got_qkv[:, 0, :, q_cols + 2 * k_cols].reshape(-1)
    gain_two = got_qkv[:, 0, :, q_cols + 2 * k_cols + 1].reshape(-1)
    q_width = query_full.shape[1]
    tokens_wide = tokens.astype(jnp.float32)
    scale_one = norm_scale(tokens_wide)
    normed_one = (tokens_wide * scale_one * gain_one.astype(jnp.float32)[None, :]).astype(
        jnp.bfloat16
    )
    query_proj = jnp.dot(normed_one, query_full, preferred_element_type=jnp.float32)
    key_projection = jnp.dot(normed_one, key_full, preferred_element_type=jnp.float32)
    value_projection = jnp.dot(normed_one, value_full, preferred_element_type=jnp.float32)
    rotated_query = apply_rotary(
        query_proj.reshape(row_count, QUERY_HEADS, HEAD_SIZE), cosine_table, sine_table
    ).astype(jnp.bfloat16)
    rotated_key = apply_rotary(
        key_projection.reshape(row_count, KEY_VALUE_HEADS, HEAD_SIZE), cosine_table, sine_table
    ).astype(jnp.bfloat16)
    value_row_slice = value_projection.astype(jnp.bfloat16).reshape(
        row_count, KEY_VALUE_HEADS, HEAD_SIZE
    )
    attended_parts = []
    lse_parts = []
    for block_index in range(n_blocks):
        starting_row = block_index * QUERY_BLOCK_ROWS
        ending_row = starting_row + QUERY_BLOCK_ROWS

        def forward_block(starting_row=starting_row, ending_row=ending_row):
            query_block_rows = rotated_query[starting_row:ending_row].reshape(
                QUERY_BLOCK_ROWS, KEY_VALUE_HEADS, heads_per_group, HEAD_SIZE
            )
            scores = block_scores(
                query_block_rows,
                rotated_key[:ending_row],
                segment[starting_row:ending_row],
                segment[:ending_row],
                starting_row,
                score_scale,
            )
            peak_score = jnp.max(scores, axis=-1, keepdims=True)
            exp_scores = jnp.exp(scores - peak_score)
            total_exp = jnp.sum(exp_scores, axis=-1, keepdims=True)
            probs_low = (exp_scores / total_exp).astype(jnp.bfloat16)
            heads_out = jnp.einsum(
                "ngtu,und->tngd",
                probs_low,
                value_row_slice[:ending_row],
                preferred_element_type=jnp.float32,
            )
            return (
                heads_out.reshape(QUERY_BLOCK_ROWS, q_width),
                (peak_score + jnp.log(total_exp))[..., 0],
            )

        heads_out, lse_block = forward_block()
        attended_parts.append(heads_out)
        lse_parts.append(lse_block)
    attended = jnp.concatenate(attended_parts, axis=0).astype(jnp.bfloat16)
    row_lse = jnp.concatenate(lse_parts, axis=2)
    got_od = gather(pack_od)
    output_full = whole_of(got_od[:, :, :q_rows])
    down_full = whole_of(got_od[:, :, q_rows:])
    branch_one = jnp.dot(attended, output_full, preferred_element_type=jnp.float32)
    hidden_mid = tokens_wide + branch_one
    got_gu = gather(pack_gu)
    f_cols = gate_weight.shape[1]
    gate_full = whole_of(got_gu[..., :f_cols])
    up_full = whole_of(got_gu[..., f_cols:])
    scale_two = norm_scale(hidden_mid)
    normed_two = (hidden_mid * scale_two * gain_two.astype(jnp.float32)[None, :]).astype(
        jnp.bfloat16
    )
    gate_proj = jnp.dot(normed_two, gate_full, preferred_element_type=jnp.float32)
    up_proj = jnp.dot(normed_two, up_full, preferred_element_type=jnp.float32)
    sigma_gate = jax.nn.sigmoid(gate_proj)
    silu_gate = gate_proj * sigma_gate
    hidden_ff = (silu_gate * up_proj).astype(jnp.bfloat16)
    branch_two = jnp.dot(hidden_ff, down_full, preferred_element_type=jnp.float32)
    mixed = (live_rows[:, None] * (hidden_mid + branch_two)).astype(jnp.bfloat16)
    gain_one_wide = gain_one.astype(jnp.float32)
    gain_two_wide = gain_two.astype(jnp.float32)
    grad_mixed = live_rows[:, None] * cotangent.astype(jnp.float32)
    grad_low = grad_mixed.astype(jnp.bfloat16)
    grad_down = jnp.einsum("tf,td->fd", hidden_ff, grad_low, preferred_element_type=jnp.float32)
    grad_hidden = jnp.einsum("td,fd->tf", grad_low, down_full, preferred_element_type=jnp.float32)
    grad_gate_low = (
        grad_hidden * up_proj * sigma_gate * (1.0 + gate_proj * (1.0 - sigma_gate))
    ).astype(jnp.bfloat16)
    grad_up_low = (grad_hidden * silu_gate).astype(jnp.bfloat16)
    grad_gate = jnp.einsum(
        "td,tf->df", normed_two, grad_gate_low, preferred_element_type=jnp.float32
    )
    grad_up = jnp.einsum("td,tf->df", normed_two, grad_up_low, preferred_element_type=jnp.float32)
    grad_normed_two = jnp.einsum(
        "tf,df->td", grad_gate_low, gate_full, preferred_element_type=jnp.float32
    )
    grad_normed_two = grad_normed_two + jnp.einsum(
        "tf,df->td", grad_up_low, up_full, preferred_element_type=jnp.float32
    )
    grad_gain_two = jnp.sum(grad_normed_two * hidden_mid * scale_two, axis=0)
    grad_mid = grad_mixed + norm_back(hidden_mid, scale_two, gain_two_wide, grad_normed_two)
    grad_branch = grad_mid.astype(jnp.bfloat16)
    grad_output = jnp.einsum("tq,td->qd", attended, grad_branch, preferred_element_type=jnp.float32)
    attention_gradient = jnp.einsum(
        "td,qd->tq", grad_branch, output_full, preferred_element_type=jnp.float32
    ).astype(jnp.bfloat16)
    query_grads = []
    key_accumulator = jnp.zeros((row_count, KEY_VALUE_HEADS, HEAD_SIZE), jnp.float32)
    value_accumulator = jnp.zeros((row_count, KEY_VALUE_HEADS, HEAD_SIZE), jnp.float32)
    for block_index in range(n_blocks):
        starting_row = block_index * QUERY_BLOCK_ROWS
        ending_row = starting_row + QUERY_BLOCK_ROWS

        def backward_block(starting_row=starting_row, ending_row=ending_row):
            query_block_rows = rotated_query[starting_row:ending_row].reshape(
                QUERY_BLOCK_ROWS, KEY_VALUE_HEADS, heads_per_group, HEAD_SIZE
            )
            block_gradient = attention_gradient[starting_row:ending_row].reshape(
                QUERY_BLOCK_ROWS, KEY_VALUE_HEADS, heads_per_group, HEAD_SIZE
            )
            scores = block_scores(
                query_block_rows,
                rotated_key[:ending_row],
                segment[starting_row:ending_row],
                segment[:ending_row],
                starting_row,
                score_scale,
            )
            attn_probs = jnp.exp(scores - row_lse[:, :, starting_row:ending_row, None])
            probs_low = attn_probs.astype(jnp.bfloat16)
            grad_probs = jnp.einsum(
                "tngd,und->ngtu",
                block_gradient,
                value_row_slice[:ending_row],
                preferred_element_type=jnp.float32,
            )
            row_dot = jnp.sum(attn_probs * grad_probs, axis=-1, keepdims=True)
            grad_scores = (attn_probs * (grad_probs - row_dot)).astype(jnp.bfloat16)
            grad_query = (
                jnp.einsum(
                    "ngtu,und->tngd",
                    grad_scores,
                    rotated_key[:ending_row],
                    preferred_element_type=jnp.float32,
                )
                * score_scale
            )
            grad_key = (
                jnp.einsum(
                    "ngtu,tngd->und",
                    grad_scores,
                    query_block_rows,
                    preferred_element_type=jnp.float32,
                )
                * score_scale
            )
            grad_value = jnp.einsum(
                "ngtu,tngd->und", probs_low, block_gradient, preferred_element_type=jnp.float32
            )
            return (
                grad_query.reshape(QUERY_BLOCK_ROWS, QUERY_HEADS, HEAD_SIZE),
                grad_key,
                grad_value,
            )

        grad_query, grad_key, grad_value = backward_block()
        query_grads.append(grad_query)
        key_accumulator = key_accumulator.at[:ending_row].add(grad_key)
        value_accumulator = value_accumulator.at[:ending_row].add(grad_value)
    grad_query_rot = jnp.concatenate(query_grads, axis=0)
    grad_query_low = (
        inverse_rotary(grad_query_rot, cosine_table, sine_table)
        .astype(jnp.bfloat16)
        .reshape(row_count, q_width)
    )
    key_gradient_reduced = (
        inverse_rotary(key_accumulator, cosine_table, sine_table)
        .astype(jnp.bfloat16)
        .reshape(row_count, KEY_VALUE_HEADS * HEAD_SIZE)
    )
    value_gradient_reduced = value_accumulator.astype(jnp.bfloat16).reshape(
        row_count, KEY_VALUE_HEADS * HEAD_SIZE
    )
    grad_qw = jnp.einsum(
        "td,tq->dq", normed_one, grad_query_low, preferred_element_type=jnp.float32
    )
    grad_kw = jnp.einsum(
        "td,tq->dq", normed_one, key_gradient_reduced, preferred_element_type=jnp.float32
    )
    grad_vw = jnp.einsum(
        "td,tq->dq", normed_one, value_gradient_reduced, preferred_element_type=jnp.float32
    )
    grad_normed_one = jnp.einsum(
        "tq,dq->td", grad_query_low, query_full, preferred_element_type=jnp.float32
    )
    grad_normed_one = grad_normed_one + jnp.einsum(
        "tq,dq->td", key_gradient_reduced, key_full, preferred_element_type=jnp.float32
    )
    grad_normed_one = grad_normed_one + jnp.einsum(
        "tq,dq->td", value_gradient_reduced, value_full, preferred_element_type=jnp.float32
    )
    grad_gain_one = jnp.sum(grad_normed_one * tokens_wide * scale_one, axis=0)
    grad_tokens = grad_mid + norm_back(tokens_wide, scale_one, gain_one_wide, grad_normed_one)
    gain_grads = jnp.stack([grad_gain_one, grad_gain_two], axis=1).reshape(
        fsdp_count, 1, q_rows, 2
    )
    gain_grads = jnp.broadcast_to(gain_grads, (fsdp_count, dp_count, q_rows, 2))
    sum_gu = scatter(jnp.concatenate([chunks_of(grad_gate), chunks_of(grad_up)], axis=3))
    sum_od = scatter(jnp.concatenate([chunks_of(grad_output), chunks_of(grad_down)], axis=2))
    sum_qkv = scatter(
        jnp.concatenate(
            [chunks_of(grad_qw), chunks_of(grad_kw), chunks_of(grad_vw), gain_grads], axis=3
        )
    )
    return (
        mixed,
        grad_tokens,
        sum_qkv[:, q_cols + 2 * k_cols],
        sum_qkv[:, :q_cols],
        sum_qkv[:, q_cols : q_cols + k_cols],
        sum_qkv[:, q_cols + k_cols : q_cols + 2 * k_cols],
        sum_od[:q_rows],
        sum_qkv[:, q_cols + 2 * k_cols + 1],
        sum_gu[:, :f_cols],
        sum_gu[:, f_cols:],
        sum_od[q_rows:],
    )


def solution(mesh):
    return jax.shard_map(
        shards,
        mesh=mesh,
        in_specs=(
            P(("fsdp", "dp"), None),
            P(("fsdp", "dp"), None),
            P("fsdp"),
            P("fsdp", "dp"),
            P("fsdp", "dp"),
            P("fsdp", "dp"),
            P("fsdp", "dp"),
            P("fsdp"),
            P("fsdp", "dp"),
            P("fsdp", "dp"),
            P("fsdp", "dp"),
            P(("fsdp", "dp"), None),
        ),
        out_specs=(
            P(("fsdp", "dp"), None),
            P(("fsdp", "dp"), None),
            P("fsdp"),
            P("fsdp", "dp"),
            P("fsdp", "dp"),
            P("fsdp", "dp"),
            P("fsdp", "dp"),
            P("fsdp"),
            P("fsdp", "dp"),
            P("fsdp", "dp"),
            P("fsdp", "dp"),
        ),
        check_vma=False,
    )
```

```python
import functools
import math
import jax
import jax.numpy as jnp
from jax import lax
from jax.experimental import pallas as pl
from jax.experimental.pallas import tpu as pltpu
from jax.sharding import Mesh
from jax.sharding import PartitionSpec as P

QUERY_HEADS = 15
KEY_VALUE_HEADS = 5
HEAD_SIZE = 64
QUERY_BLOCK = 256
ROW_BLOCK = 256
SEGMENT_ROWS = 16
epsilon = 1e-05
rope_base = 100000.0
masked_fill = -1e30


def product(left, right):
    return jnp.dot(left, right, preferred_element_type=jnp.float32)


def stacked_split(row):
    high = row.astype(jnp.bfloat16).astype(jnp.float32)
    middle = (row - high).astype(jnp.bfloat16).astype(jnp.float32)
    low = row - high - middle
    place = lax.broadcasted_iota(jnp.int32, (SEGMENT_ROWS, row.shape[1]), 0)
    return jnp.where(
        place == 0, high, jnp.where(place == 1, middle, jnp.where(place == 2, low, 0.0))
    ).astype(jnp.bfloat16)


def causal(block):
    key_place = lax.broadcasted_iota(jnp.int32, (block, block), 0)
    query_place = lax.broadcasted_iota(jnp.int32, (block, block), 1)
    return key_place <= query_place


def attention_forward_kernel(onehot_ref, penalty_ref, q_ref, k_ref, v_ref, o_ref, lse_ref, key_rows):
    rows = q_ref.shape[1]
    block = min(QUERY_BLOCK, rows)
    filler = jnp.zeros((HEAD_SIZE - SEGMENT_ROWS, rows), jnp.bfloat16)
    key_rows[...] = jnp.concatenate([k_ref[...], onehot_ref[...], filler], axis=0).T
    allowed = causal(block)
    lse_ref[...] = jnp.zeros_like(lse_ref)
    for i in range(rows // block):
        start, stop = i * block, (i + 1) * block
        for h in range(q_ref.shape[0] // HEAD_SIZE):
            q_side = jnp.concatenate(
                [
                    q_ref[h * HEAD_SIZE : (h + 1) * HEAD_SIZE, start:stop],
                    penalty_ref[:, start:stop],
                    filler[:, :block],
                ],
                axis=0,
            )
            near = jnp.where(allowed, product(key_rows[start:stop], q_side), masked_fill)
            peak = jnp.max(near, axis=0, keepdims=True)
            if i:
                far = product(key_rows[:start], q_side)
                peak = jnp.maximum(peak, jnp.max(far, axis=0, keepdims=True))
            near = jnp.exp(near - peak)
            total = jnp.sum(near, axis=0, keepdims=True)
            out = product(v_ref[:, start:stop], near.astype(jnp.bfloat16))
            if i:
                far = jnp.exp(far - peak)
                total = total + jnp.sum(far, axis=0, keepdims=True)
                out = out + product(v_ref[:, :start], far.astype(jnp.bfloat16))
            o_ref[h * HEAD_SIZE : (h + 1) * HEAD_SIZE, start:stop] = (out / total).astype(
                jnp.bfloat16
            )
            lse_ref[0, h : h + 1, start:stop] = peak + jnp.log(total)


def attention_backward_kernel(
    onehot_ref, penalty_ref, cos_ref, sin_ref, q_ref, k_ref, v_ref, o_ref, do_ref, lse_ref,
    dq_ref, dk_ref, dv_ref, key_rows, value_rows, pair_rows, weights, sums,
):
    rows = q_ref.shape[1]
    block = min(QUERY_BLOCK, rows)
    heads = q_ref.shape[0] // HEAD_SIZE
    half = HEAD_SIZE // 2
    scale = 1.0 / math.sqrt(HEAD_SIZE)
    ones = jnp.ones((SEGMENT_ROWS, rows), jnp.bfloat16)
    zeros = jnp.zeros((HEAD_SIZE, rows), jnp.bfloat16)
    short = zeros[: HEAD_SIZE - 2 * SEGMENT_ROWS]
    long = zeros[: HEAD_SIZE - SEGMENT_ROWS]
    key_rows[...] = jnp.concatenate([k_ref[...], onehot_ref[...], ones, short], axis=0).T
    value_rows[...] = jnp.concatenate([v_ref[...], ones, long], axis=0).T
    count = rows // block
    for h in range(heads):
        q_rows = jnp.concatenate([q_ref[h * HEAD_SIZE : (h + 1) * HEAD_SIZE], zeros], axis=0).T
        do_rows = jnp.concatenate([zeros, do_ref[h * HEAD_SIZE : (h + 1) * HEAD_SIZE]], axis=0).T
        for i in range(count):
            pair_rows[i, 2 * h * block : (2 * h + 1) * block] = q_rows[i * block : (i + 1) * block]
            pair_rows[i, (2 * h + 1) * block : (2 * h + 2) * block] = do_rows[
                i * block : (i + 1) * block
            ]
    allowed = causal(block)

    def back(w):
        return w[:half], w[half:]

    for i in reversed(range(count)):
        start, stop = i * block, (i + 1) * block
        cos, sin = cos_ref[:, start:stop], sin_ref[:, start:stop]
        for h in range(heads):
            own = slice(h * HEAD_SIZE, (h + 1) * HEAD_SIZE)
            do = do_ref[own, start:stop]
            delta = jnp.sum(
                do.astype(jnp.float32) * o_ref[own, start:stop].astype(jnp.float32),
                axis=0, keepdims=True,
            )
            q_side = jnp.concatenate(
                [
                    q_ref[own, start:stop], penalty_ref[:, start:stop],
                    stacked_split(-lse_ref[0, h : h + 1, start:stop]), short[:, :block],
                ],
                axis=0,
            )
            do_side = jnp.concatenate([do, stacked_split(-delta), long[:, :block]], axis=0)
            left, middle, right = 2 * h * block, (2 * h + 1) * block, (2 * h + 2) * block
            probs = jnp.exp(
                jnp.where(allowed, product(key_rows[start:stop], q_side), masked_fill)
            )
            grads = (probs * product(value_rows[start:stop], do_side)).astype(jnp.bfloat16)
            weights[start:stop, left:middle] = grads
            weights[start:stop, middle:right] = probs.astype(jnp.bfloat16)
            dq = product(k_ref[:, start:stop], grads)
            if i:
                probs = jnp.exp(product(key_rows[:start], q_side))
                grads = (probs * product(value_rows[:start], do_side)).astype(jnp.bfloat16)
                weights[:start, left:middle] = grads
                weights[:start, middle:right] = probs.astype(jnp.bfloat16)
                dq = dq + product(k_ref[:, :start], grads)
            w1, w2 = back(dq * scale)
            dq_ref[h * HEAD_SIZE : h * HEAD_SIZE + half, start:stop] = (
                w1 * cos + w2 * sin
            ).astype(jnp.bfloat16)
            dq_ref[h * HEAD_SIZE + half : (h + 1) * HEAD_SIZE, start:stop] = (
                w2 * cos - w1 * sin
            ).astype(jnp.bfloat16)
        part = product(weights[:stop], pair_rows[i])
        if i == count - 1:
            sums[...] = part
        else:
            sums[:stop] = sums[:stop] + part
    both = sums[...].T
    w1, w2 = back(both[:HEAD_SIZE])
    cos, sin = cos_ref[...], sin_ref[...]
    dk_ref[:half] = (w1 * cos + w2 * sin).astype(jnp.bfloat16)
    dk_ref[half:] = (w2 * cos - w1 * sin).astype(jnp.bfloat16)
    dv_ref[...] = both[HEAD_SIZE:].astype(jnp.bfloat16)


def attention_specs(rows, low=0):
    group = QUERY_HEADS // KEY_VALUE_HEADS * HEAD_SIZE
    whole = pl.BlockSpec((SEGMENT_ROWS, rows), lambda g: (0, 0))
    table = pl.BlockSpec((HEAD_SIZE // 2, rows), lambda g: (0, 0))
    wide = pl.BlockSpec((group, rows), lambda g: (g + low, 0))
    narrow = pl.BlockSpec((HEAD_SIZE, rows), lambda g: (g + low, 0))
    lse = pl.BlockSpec((1, 8, rows), lambda g: (g + low, 0, 0))
    return whole, table, wide, narrow, lse


def attention_forward(onehot, penalty, q, k, v):
    rows = q.shape[1]
    whole, table, wide, narrow, lse = attention_specs(rows)
    return pl.pallas_call(
        attention_forward_kernel,
        grid=(KEY_VALUE_HEADS,),
        in_specs=[whole, whole, wide, narrow, narrow],
        out_specs=[wide, lse],
        out_shape=[
            jax.ShapeDtypeStruct(q.shape, jnp.bfloat16),
            jax.ShapeDtypeStruct((KEY_VALUE_HEADS, 8, rows), jnp.float32),
        ],
        scratch_shapes=[pltpu.VMEM((rows, 2 * HEAD_SIZE), jnp.bfloat16)],
        compiler_params=pltpu.CompilerParams(vmem_limit_bytes=32 << 20),
        cost_estimate=pl.CostEstimate(
            flops=8 * 1153 * 10**6 * 2, transcendentals=0, bytes_accessed=8 << 20
        ),
        name="attention_forward",
    )(onehot, penalty, q, k, v)


def attention_backward(onehot, penalty, cos, sin, q, k, v, o, do, lse_rows, low, count):
    rows = q.shape[1]
    block = min(QUERY_BLOCK, rows)
    heads = QUERY_HEADS // KEY_VALUE_HEADS
    whole, table, wide, narrow, lse = attention_specs(rows, low)
    _, _, wide_out, narrow_out, _ = attention_specs(rows)
    return pl.pallas_call(
        attention_backward_kernel,
        grid=(count,),
        in_specs=[whole, whole, table, table, wide, narrow, narrow, wide, wide, lse],
        out_specs=[wide_out, narrow_out, narrow_out],
        out_shape=[
            jax.ShapeDtypeStruct((count * size, rows), jnp.bfloat16)
            for size in (heads * HEAD_SIZE, HEAD_SIZE, HEAD_SIZE)
        ],
        scratch_shapes=[
            pltpu.VMEM((rows, 2 * HEAD_SIZE), jnp.bfloat16),
            pltpu.VMEM((rows, 2 * HEAD_SIZE), jnp.bfloat16),
            pltpu.VMEM((rows // block, 2 * heads * block, 2 * HEAD_SIZE), jnp.bfloat16),
            pltpu.VMEM((rows, 2 * heads * block), jnp.bfloat16),
            pltpu.VMEM((rows, 2 * HEAD_SIZE), jnp.float32),
        ],
        compiler_params=pltpu.CompilerParams(vmem_limit_bytes=40 << 20),
        cost_estimate=pl.CostEstimate(
            flops=count * 6 * 1153 * 10**6, transcendentals=0, bytes_accessed=count * 5 << 19
        ),
        name="attention_backward",
    )(onehot, penalty, cos, sin, q, k, v, o, do, lse_rows)


def product_nt(left, right):
    return lax.dot_general(
        left, right, (((1,), (1,)), ((), ())), preferred_element_type=jnp.float32
    )


def contract(left, right, left_dim, right_dim):
    return lax.dot_general(
        left, right, (((left_dim,), (right_dim,)), ((), ())), preferred_element_type=jnp.float32
    )


def assemble_kernel(cuts, place_ref, *refs):
    units, outs, sems = refs[:8], refs[8:-1], refs[-1]
    copies = []
    for unit in range(8):
        y = place_ref[0] ^ (unit >> 2)
        d = (place_ref[1] ^ ((unit >> 1) & 1)) * 2 + (place_ref[2] ^ (unit & 1))
        for at, (low, high) in enumerate(cuts):
            copies.append(
                pltpu.make_async_copy(
                    units[unit].at[:, low:high], outs[at].at[d, :, y], sems.at[unit, at]
                )
            )
    for copy in copies:
        copy.start()
    for copy in copies:
        copy.wait()


def assemble_unaligned(place, units, rows):
    whole = jnp.stack(units).reshape((2, 2, 2) + units[0].shape)
    for axis in range(3):
        whole = jnp.where(place[axis] == 0, whole, jnp.flip(whole, axis))
    whole = whole.transpose(1, 2, 3, 0, 4, 5)
    cuts = [sum(rows[:i]) for i in range(len(rows) + 1)]
    parts = [whole[:, :, :, :, low:high] for low, high in zip(cuts, cuts[1:])]
    return [part.reshape(4, -1, part.shape[-1]) for part in parts]


def assemble(place, units, rows):
    nz, total, width = units[0].shape
    if any(r % 8 for r in rows) or any(r % 16 for r in rows[:-1]):
        return assemble_unaligned(place, units, rows)
    cuts = [(sum(rows[:i]), sum(rows[: i + 1])) for i in range(len(rows))]
    outs = pl.pallas_call(
        functools.partial(assemble_kernel, cuts),
        grid_spec=pltpu.PrefetchScalarGridSpec(
            num_scalar_prefetch=1,
            grid=(1,),
            in_specs=[pl.BlockSpec(memory_space=pl.ANY)] * 8,
            out_specs=[pl.BlockSpec(memory_space=pl.ANY)] * len(cuts),
            scratch_shapes=[pltpu.SemaphoreType.DMA((8, len(cuts)))],
        ),
        out_shape=[jax.ShapeDtypeStruct((4, nz, 2, r, width), jnp.bfloat16) for r in rows],
        compiler_params=pltpu.CompilerParams(vmem_limit_bytes=4 << 20),
        cost_estimate=pl.CostEstimate(
            flops=0, transcendentals=0, bytes_accessed=2 * 8 * nz * total * width * 2
        ),
        name="assemble",
    )(place, *units)
    return [out.reshape(4, nz * 2 * r, width) for out, r in zip(outs, rows)]


def feed_forward_kernel(
    place_ref, n2_ref, gy_ref, down_ref, *refs
):
    units = refs[:-12]
    (mixed_ref, dn2_ref, gu_send_ref, gu_keep_ref, od_send_ref, od_keep_ref) = refs[-12:-6]
    pieces, weights, n2_across, grads, hidden, sems = refs[-6:]
    step = pl.program_id(0)
    rows, width = n2_ref.shape
    nz, unit_rows, double = units[0].shape
    ff = double // 2
    block = min(ROW_BLOCK, rows)

    def copies(at):
        xr, cr = 1 - at % 2, 1 - at // 2
        made = []
        if len(units) == 1:
            whole = units[0].at[(place_ref[1] ^ xr) * 2 + (place_ref[2] ^ cr)]
            return [pltpu.make_async_copy(whole, pieces.at[at, 0], sems.at[at, 0])]
        for yr in range(2):
            y = place_ref[0] ^ yr
            for z in range(nz):
                made.append(
                    pltpu.make_async_copy(
                        units[yr * 4 + xr * 2 + cr].at[z],
                        pieces.at[at, 2 * z + y],
                        sems.at[at, yr * nz + z],
                    )
                )
        return made

    @pl.when(step == 0)
    def _():
        for at in range(4):
            for copy in copies(at):
                copy.start()
        n2_across[...] = n2_ref[...].T
        mixed_ref[...] = jnp.zeros_like(mixed_ref)
        dn2_ref[...] = jnp.zeros_like(dn2_ref)

    for at in range(4):

        @pl.when(step == at)
        def _():
            for copy in copies(at):
                copy.wait()

    for f in range(pieces.shape[1]):
        weights[f * pieces.shape[2] : (f + 1) * pieces.shape[2]] = pieces[step, f]

    def chunk(i, carry):
        part = pl.ds(pl.multiple_of(i * block, block), block)
        n2 = n2_ref[part]
        gate = product(n2, weights[:, :ff])
        up = product(n2, weights[:, ff:])
        sigma = jax.nn.sigmoid(gate)
        silu = gate * sigma
        hid = (silu * up).astype(jnp.bfloat16)
        hidden[part] = hid
        dhid = product_nt(gy_ref[0, part], down_ref[0])
        for d in range(1, 4):
            dhid = dhid + product_nt(gy_ref[d, part], down_ref[d])
        grads[part, :ff] = (dhid * up * (sigma * (1.0 + gate * (1.0 - sigma)))).astype(
            jnp.bfloat16
        )
        grads[part, ff:] = (dhid * silu).astype(jnp.bfloat16)
        for d in range(4):
            mixed_ref[d, part] = mixed_ref[d, part] + product(hid, down_ref[d])
        dn2_ref[part] = dn2_ref[part] + product_nt(grads[part], weights[...])
        return carry

    lax.fori_loop(0, rows // block, chunk, 0)

    def weight_grads(out_ref):
        for low in range(0, double, 256):
            out_ref[0, :, low : low + 256] = product(
                n2_across[...], grads[:, low : low + 256]
            ).astype(jnp.bfloat16)

    @pl.when(step < 2)
    def _():
        weight_grads(gu_send_ref)

    @pl.when(step >= 2)
    def _():
        weight_grads(gu_keep_ref)

    hidden_across = hidden[...].T
    own = od_send_ref.shape[1]
    depth = ff // own
    for cr, out_ref in ((1, od_send_ref), (0, od_keep_ref)):
        for k in range(2):
            d = (place_ref[1] ^ (1 - k)) * 2 + (place_ref[2] ^ cr)
            value = product(hidden_across, gy_ref[d]).astype(jnp.bfloat16)
            for f in range(own):
                out_ref[k, f, :depth] = value[f * depth : (f + 1) * depth]


def feed_forward(place, n2, gy, down, units, od_rows):
    rows, width = n2.shape
    fsdp, depth = 2 * units[0].shape[0], units[0].shape[1]
    if depth % 8:
        units = assemble(place, units, [depth])
        depth = width
    double = units[0].shape[2]
    ff = double // 2
    d_cols = gy.shape[2]
    own = fsdp // 4

    def hidden_block(s, place_ref):
        return (place_ref[1] ^ (1 - s % 2)) * 2 + (place_ref[2] ^ (1 - s // 2))

    once = pl.Buffered(1)
    flops = 2 * rows * width * 4 * ff * 9
    return pl.pallas_call(
        feed_forward_kernel,
        grid_spec=pltpu.PrefetchScalarGridSpec(
            num_scalar_prefetch=1,
            grid=(4,),
            in_specs=[
                pl.BlockSpec((rows, width), lambda s, p: (0, 0), pipeline_mode=once),
                pl.BlockSpec((4, rows, d_cols), lambda s, p: (0, 0, 0), pipeline_mode=once),
                pl.BlockSpec((4, ff, d_cols), lambda s, p: (0, hidden_block(s, p), 0)),
            ]
            + [pl.BlockSpec(memory_space=pl.ANY)] * len(units),
            out_specs=[
                pl.BlockSpec((4, rows, d_cols), lambda s, p: (0, 0, 0), pipeline_mode=once),
                pl.BlockSpec((rows, width), lambda s, p: (0, 0), pipeline_mode=once),
                pl.BlockSpec((1, width, double), lambda s, p: (jnp.minimum(s, 1), 0, 0)),
                pl.BlockSpec((1, width, double), lambda s, p: (jnp.maximum(s - 2, 0), 0, 0)),
                pl.BlockSpec((2, own, od_rows, d_cols), lambda s, p: (0, hidden_block(s, p), 0, 0)),
                pl.BlockSpec((2, own, od_rows, d_cols), lambda s, p: (0, hidden_block(s, p), 0, 0)),
            ],
            scratch_shapes=[
                pltpu.VMEM((4, width // depth, depth, double), jnp.bfloat16),
                pltpu.VMEM((width, double), jnp.bfloat16),
                pltpu.VMEM((width, rows), jnp.bfloat16),
                pltpu.VMEM((rows, double), jnp.bfloat16),
                pltpu.VMEM((rows, ff), jnp.bfloat16),
                pltpu.SemaphoreType.DMA((4, fsdp)),
            ],
        ),
        out_shape=[
            jax.ShapeDtypeStruct((4, rows, d_cols), jnp.float32),
            jax.ShapeDtypeStruct((rows, width), jnp.float32),
            jax.ShapeDtypeStruct((2, width, double), jnp.bfloat16),
            jax.ShapeDtypeStruct((2, width, double), jnp.bfloat16),
            jax.ShapeDtypeStruct((2, fsdp, od_rows, d_cols), jnp.bfloat16),
            jax.ShapeDtypeStruct((2, fsdp, od_rows, d_cols), jnp.bfloat16),
        ],
        compiler_params=pltpu.CompilerParams(vmem_limit_bytes=60 << 20),
        cost_estimate=pl.CostEstimate(flops=flops, transcendentals=0, bytes_accessed=48 << 20),
        name="feed_forward",
    )(place, n2, gy, down, *units)


def after(value, *others):
    return lax.optimization_barrier((value, *others))[0]


def swap(value, axes):
    count = 2 ** len(axes)
    return lax.ppermute(value, axes, [(i, count - 1 - i) for i in range(count)])


def z_partner(value, mask, nz):
    return lax.ppermute(value, "z", [(i, i ^ mask) for i in range(nz)])


def gather_z(shard, nz):
    if nz != 4:
        return lax.all_gather(shard, "z", axis=0, tiled=False)
    me = lax.axis_index("z")
    unit = jnp.zeros((nz,) + shard.shape, shard.dtype)
    for mask in range(nz):
        piece = z_partner(shard, mask, nz) if mask else shard
        unit = lax.dynamic_update_slice(unit, piece[None], (me ^ mask,) + (0,) * shard.ndim)
    return unit


def scatter_z(unit, nz):
    if nz != 4:
        return lax.psum_scatter(unit, "z", scatter_dimension=0, tiled=False).astype(jnp.float32)
    me = lax.axis_index("z")

    def part(mask):
        return lax.dynamic_index_in_dim(unit, me ^ mask, 0, keepdims=False)

    total = part(0).astype(jnp.float32)
    for mask in range(1, nz):
        total = total + z_partner(part(mask), mask, nz).astype(jnp.float32)
    return total


def units_of(own, along_y, along_x, along_both):
    four = (own, along_x, along_y, along_both)
    across = [swap(unit, ("c",)) for unit in four]
    order = []
    for yr in range(2):
        for xr in range(2):
            order += [four[yr * 2 + xr], across[yr * 2 + xr]]
    return order


def norm_back(values, scale_rows, gain_wide, upstream):
    weighted = gain_wide[None, :] * upstream
    return scale_rows * weighted - values * scale_rows**3 * jnp.mean(
        weighted * values, axis=1, keepdims=True
    )


def norm_scale(values):
    return lax.rsqrt(jnp.mean(values * values, axis=1, keepdims=True) + epsilon)


def shards(
    tokens,
    seq_lengths,
    norm1_gain,
    q_weight,
    k_weight,
    v_weight,
    o_weight,
    norm2_gain,
    gate_weight,
    up_weight,
    down_weight,
    cotangent,
):
    f32, bf16 = jnp.float32, jnp.bfloat16
    rows, width = tokens.shape
    nz = lax.axis_size("z")
    me_z, me_y, me_x, me_c = (lax.axis_index(a) for a in ("z", "y", "x", "c"))
    place = jnp.stack([me_y, me_x, me_c]).astype(jnp.int32)
    r_in, q_cols = q_weight.shape
    k_cols = k_weight.shape[1]
    qkv = q_cols + 2 * k_cols
    lanes = -(-(qkv + 2) // 128) * 128
    down_rows = down_weight.shape[0]
    o_rows = o_weight.shape[0]
    ff = gate_weight.shape[1]

    pack_a = jnp.concatenate(
        [
            q_weight,
            k_weight,
            v_weight,
            norm1_gain[:, None],
            norm2_gain[:, None],
            jnp.zeros((r_in, lanes - qkv - 2), bf16),
        ],
        axis=1,
    )
    filler = -(down_rows + o_rows) % 16
    pack_od = jnp.pad(jnp.concatenate([down_weight, o_weight], axis=0), ((0, filler), (0, 0)))
    pack_gu = jnp.concatenate([gate_weight, up_weight], axis=1)
    unit_a = gather_z(pack_a, nz)
    units_a = units_of(
        unit_a, swap(unit_a, ("y",)), swap(unit_a, ("x",)), swap(unit_a, ("y", "x"))
    )
    [weights_a] = assemble(place, units_a, [r_in])
    unit_od = gather_z(after(pack_od, unit_a), nz)
    unit_gu = gather_z(after(pack_gu, unit_a), nz)
    od_y, od_x = swap(unit_od, ("y",)), swap(unit_od, ("x",))
    gu_y, gu_x = swap(unit_gu, ("y",)), swap(unit_gu, ("x",))
    gain_one = weights_a[0, :, qkv].astype(f32)
    gain_two = weights_a[0, :, qkv + 1].astype(f32)

    lengths = seq_lengths[0]
    slots = jnp.arange(lengths.shape[0])
    ends = jnp.sum(jnp.where(slots[None, :] <= slots[:, None], lengths[None, :], 0), axis=1)
    places = jnp.arange(rows, dtype=jnp.int32)
    passed = (places[None, :] >= ends[:, None]).astype(jnp.int32)
    segment = jnp.sum(passed, axis=0)
    position = places - jnp.sum(passed * lengths[:, None], axis=0)
    live = (places < ends[-1]).astype(f32)
    same = jnp.arange(SEGMENT_ROWS)[:, None] == segment[None, :]
    onehot = same.astype(bf16)
    penalty = jnp.where(same, 0.0, masked_fill).astype(bf16)
    half = HEAD_SIZE // 2
    inverse = jnp.exp(
        -math.log(rope_base) * (jnp.arange(half, dtype=f32) * (2.0 / HEAD_SIZE))
    )
    angle = inverse[:, None] * position.astype(f32)[None, :]
    cos, sin = jnp.cos(angle), jnp.sin(angle)

    x = tokens.astype(f32)
    scale_one = norm_scale(x)
    n1 = (x * scale_one * gain_one[None, :]).astype(bf16)
    proj = lax.dot_general(
        weights_a, n1, (((1,), (1,)), ((), ())), preferred_element_type=f32
    )
    q_across = proj[:, :q_cols].reshape(QUERY_HEADS, 2, half, rows)
    k_across = proj[:, q_cols : q_cols + k_cols].reshape(KEY_VALUE_HEADS, 2, half, rows)
    v_across = proj[:, q_cols + k_cols : qkv].reshape(-1, rows).astype(bf16)

    def rope(u):
        u1, u2 = u[:, 0], u[:, 1]
        return (
            jnp.stack([u1 * cos - u2 * sin, u2 * cos + u1 * sin], axis=1)
            .astype(bf16)
            .reshape(-1, rows)
        )

    qr = rope(q_across) * jnp.asarray(1.0 / math.sqrt(HEAD_SIZE), bf16)
    kr = rope(k_across)
    qr = after(qr, unit_od, unit_gu)
    att, lse = attention_forward(onehot, penalty, qr, kr, v_across)
    od_y, od_x, gu_y, gu_x = (after(a, att) for a in (od_y, od_x, gu_y, gu_x))
    units_od = units_of(unit_od, od_y, od_x, swap(od_y, ("x",)))
    units_gu = units_of(unit_gu, gu_y, gu_x, swap(gu_x, ("y",)))
    down_all, o_all = assemble(place, units_od, [down_rows, o_rows + filler])
    o_all = o_all.reshape(4, 2 * nz, o_rows + filler, -1)[:, :, :o_rows].reshape(4, width, -1)
    o_full = jnp.concatenate([o_all[d] for d in range(4)], axis=1)
    hmid = x + contract(att, o_full, 0, 0)

    scale_two = norm_scale(hmid)
    n2 = (hmid * scale_two * gain_two[None, :]).astype(bf16)
    gy = live[:, None] * cotangent.astype(f32)
    d_cols = width // 4
    gy_low = gy.astype(bf16)
    gy_parts = jnp.stack([gy_low[:, d * d_cols : (d + 1) * d_cols] for d in range(4)])
    mixed_parts, dn2, gu_send, gu_keep, od_send, od_keep = feed_forward(
        place, n2, gy_parts, down_all, units_gu, down_rows + o_rows + filler
    )
    mixed = (
        live[:, None] * (hmid + jnp.concatenate([mixed_parts[d] for d in range(4)], axis=1))
    ).astype(bf16)
    grad_gain_two = jnp.sum(dn2 * hmid * scale_two, axis=0)
    dh = gy + norm_back(hmid, scale_two, gain_two, dn2)
    da = dh.astype(bf16)

    def quarter(halves, k, y):
        return lax.dynamic_index_in_dim(halves[k], y, 1, keepdims=False)

    gu_shape = (2, nz, 2, r_in, 2 * ff)
    gu_keep = gu_keep.reshape(gu_shape)
    gu_got = swap(gu_send, ("c",)).reshape(gu_shape)

    def both_gu(k, y):
        return quarter(gu_keep, k, y) + quarter(gu_got, k, y)

    gu_first = both_gu(0, 1 - me_y)
    gu_x = both_gu(0, me_y) + swap(gu_first, ("y",))
    gu_unit = both_gu(1, me_y) + swap(both_gu(1, 1 - me_y), ("y",)) + swap(gu_x, ("x",))
    sum_gu = scatter_z(gu_unit, nz)

    da_parts = jnp.stack([da[:, d * d_cols : (d + 1) * d_cols] for d in range(4)])
    grad_o = lax.dot_general(
        da_parts, att, (((1,), (1,)), ((), ())), preferred_element_type=f32
    )
    grad_o = grad_o.transpose(0, 2, 1).astype(bf16).reshape(2, 2, 2 * nz, o_rows, d_cols)
    datt = contract(o_full, da, 1, 1).astype(bf16)

    def with_o(parts, c):
        own = lax.dynamic_index_in_dim(grad_o, c, 1, keepdims=False)
        own = jnp.stack(
            [
                lax.dynamic_index_in_dim(own, 1 - me_x, 0, keepdims=False),
                lax.dynamic_index_in_dim(own, me_x, 0, keepdims=False),
            ]
        )
        return lax.dynamic_update_slice(parts, own, (0, 0, down_rows, 0))

    od_shape = (2, nz, 2, down_rows + o_rows + filler, d_cols)
    od_got = swap(with_o(od_send, 1 - me_c), ("c",)).reshape(od_shape)
    od_keep = with_o(od_keep, me_c).reshape(od_shape)

    def both_od(k, y):
        return quarter(od_keep, k, y) + quarter(od_got, k, y)

    od_first = both_od(0, 1 - me_y)
    od_y = both_od(1, 1 - me_y) + swap(od_first, ("x",))
    od_unit = both_od(1, me_y) + swap(both_od(0, me_y), ("x",)) + swap(od_y, ("y",))
    sum_od = scatter_z(od_unit, nz)

    back = functools.partial(attention_backward, onehot, penalty, cos, sin, qr, kr, v_across, att)
    first = back(after(datt, gu_first), lse, 0, 2)
    second = back(after(datt, od_first, first[0]), lse, 2, 3)
    dq, dk, dv = (jnp.concatenate(pair) for pair in zip(first, second))
    dproj = jnp.concatenate(
        [
            dq.reshape(4, q_cols, rows),
            dk.reshape(4, k_cols, rows),
            dv.reshape(4, k_cols, rows),
            jnp.zeros((4, lanes - qkv, rows), bf16),
        ],
        axis=1,
    )
    grad_a = lax.dot_general(dproj, n1, (((2,), (0,)), ((), ())), preferred_element_type=f32)
    grad_a = grad_a.transpose(0, 2, 1).astype(bf16).reshape(2, 2, nz, 2, r_in, lanes)
    a_send = lax.dynamic_index_in_dim(grad_a, 1 - me_c, 1, keepdims=False)
    a_keep = lax.dynamic_index_in_dim(grad_a, me_c, 1, keepdims=False)
    dn1 = lax.dot_general(
        dproj, weights_a, (((0, 1), (0, 2)), ((), ())), preferred_element_type=f32
    )
    gains = jnp.stack([jnp.sum(dn1 * x * scale_one, axis=0), grad_gain_two], axis=1)
    gains = (gains + swap(gains.astype(bf16), ("c",)).astype(f32)).astype(bf16)
    gains = jnp.pad(gains, ((0, 0), (qkv, lanes - qkv - 2)))
    gains = gains.reshape(1, nz, 2, r_in, lanes)
    a_sum = a_keep + swap(a_send, ("c",)) + gains

    def part_a(x, y):
        return lax.dynamic_index_in_dim(
            lax.dynamic_index_in_dim(a_sum, x, 0, keepdims=False), y, 1, keepdims=False
        )

    a_unit = (
        part_a(me_x, me_y)
        + swap(part_a(1 - me_x, me_y), ("x",))
        + swap(part_a(me_x, 1 - me_y), ("y",))
        + swap(part_a(1 - me_x, 1 - me_y), ("y", "x"))
    )
    sum_a = scatter_z(a_unit, nz)
    grad_tokens = dh + norm_back(x, scale_one, gain_one, dn1)
    return (
        mixed,
        grad_tokens,
        sum_a[:, qkv],
        sum_a[:, :q_cols],
        sum_a[:, q_cols : q_cols + k_cols],
        sum_a[:, q_cols + k_cols : qkv],
        sum_od[down_rows : down_rows + o_rows],
        sum_a[:, qkv + 1],
        sum_gu[:, :ff],
        sum_gu[:, ff:],
        sum_od[:down_rows],
    )


def solution(mesh):
    fsdp, dp = mesh.devices.shape
    assert dp == 4 and fsdp % 2 == 0
    split = Mesh(mesh.devices.reshape(fsdp // 2, 2, 2, 2), ("z", "y", "x", "c"))
    rows, grid, gain = P(("z", "y", "x", "c"), None), P(("z", "y"), ("x", "c")), P(("z", "y"))
    return jax.shard_map(
        shards,
        mesh=split,
        in_specs=(rows, rows, gain, grid, grid, grid, grid, gain, grid, grid, grid, rows),
        out_specs=(rows, rows, gain, grid, grid, grid, grid, gain, grid, grid, grid),
        check_vma=False,
    )
```

```python
import functools
import math
import jax
import jax.numpy as jnp
from jax import lax
from jax.experimental import pallas as pl
from jax.experimental.pallas import tpu as pltpu
from jax.sharding import Mesh
from jax.sharding import PartitionSpec as P

QUERY_HEADS = 15
KEY_VALUE_HEADS = 5
HEAD_SIZE = 64
QUERY_BLOCK = 256
ROW_BLOCK = 512
SEGMENT_ROWS = 16
epsilon = 1e-05
rope_base = 100000.0
masked_fill = -1e30


def product(left, right):
    return jnp.dot(left, right, preferred_element_type=jnp.float32)


def stacked_split(row):
    high = row.astype(jnp.bfloat16).astype(jnp.float32)
    middle = (row - high).astype(jnp.bfloat16).astype(jnp.float32)
    low = row - high - middle
    place = lax.broadcasted_iota(jnp.int32, (SEGMENT_ROWS, row.shape[1]), 0)
    return jnp.where(
        place == 0, high, jnp.where(place == 1, middle, jnp.where(place == 2, low, 0.0))
    ).astype(jnp.bfloat16)


def causal(block):
    key_place = lax.broadcasted_iota(jnp.int32, (block, block), 0)
    query_place = lax.broadcasted_iota(jnp.int32, (block, block), 1)
    return key_place <= query_place


def attention_forward_kernel(onehot_ref, penalty_ref, q_ref, k_ref, v_ref, o_ref, lse_ref, key_rows):
    rows = q_ref.shape[1]
    block = min(QUERY_BLOCK, rows)
    filler = jnp.zeros((HEAD_SIZE - SEGMENT_ROWS, rows), jnp.bfloat16)
    key_rows[...] = jnp.concatenate([k_ref[...], onehot_ref[...], filler], axis=0).T
    allowed = causal(block)
    lse_ref[...] = jnp.zeros_like(lse_ref)
    for i in range(rows // block):
        start, stop = i * block, (i + 1) * block
        for h in range(q_ref.shape[0] // HEAD_SIZE):
            q_side = jnp.concatenate(
                [
                    q_ref[h * HEAD_SIZE : (h + 1) * HEAD_SIZE, start:stop],
                    penalty_ref[:, start:stop],
                    filler[:, :block],
                ],
                axis=0,
            )
            near = jnp.where(allowed, product(key_rows[start:stop], q_side), masked_fill)
            peak = jnp.max(near, axis=0, keepdims=True)
            if i:
                far = product(key_rows[:start], q_side)
                peak = jnp.maximum(peak, jnp.max(far, axis=0, keepdims=True))
            near = jnp.exp(near - peak)
            total = jnp.sum(near, axis=0, keepdims=True)
            out = product(v_ref[:, start:stop], near.astype(jnp.bfloat16))
            if i:
                far = jnp.exp(far - peak)
                total = total + jnp.sum(far, axis=0, keepdims=True)
                out = out + product(v_ref[:, :start], far.astype(jnp.bfloat16))
            o_ref[h * HEAD_SIZE : (h + 1) * HEAD_SIZE, start:stop] = (out / total).astype(
                jnp.bfloat16
            )
            lse_ref[0, h : h + 1, start:stop] = peak + jnp.log(total)


def attention_backward_kernel(
    onehot_ref, penalty_ref, cos_ref, sin_ref, q_ref, k_ref, v_ref, o_ref, do_ref, lse_ref,
    dq_ref, dk_ref, dv_ref, key_rows, value_rows, pair_rows, weights, sums,
):
    rows = q_ref.shape[1]
    block = min(QUERY_BLOCK, rows)
    heads = q_ref.shape[0] // HEAD_SIZE
    half = HEAD_SIZE // 2
    scale = 1.0 / math.sqrt(HEAD_SIZE)
    ones = jnp.ones((SEGMENT_ROWS, rows), jnp.bfloat16)
    zeros = jnp.zeros((HEAD_SIZE, rows), jnp.bfloat16)
    short = zeros[: HEAD_SIZE - 2 * SEGMENT_ROWS]
    long = zeros[: HEAD_SIZE - SEGMENT_ROWS]
    key_rows[...] = jnp.concatenate([k_ref[...], onehot_ref[...], ones, short], axis=0).T
    value_rows[...] = jnp.concatenate([v_ref[...], ones, long], axis=0).T
    count = rows // block
    for h in range(heads):
        q_rows = jnp.concatenate([q_ref[h * HEAD_SIZE : (h + 1) * HEAD_SIZE], zeros], axis=0).T
        do_rows = jnp.concatenate([zeros, do_ref[h * HEAD_SIZE : (h + 1) * HEAD_SIZE]], axis=0).T
        for i in range(count):
            pair_rows[i, 2 * h * block : (2 * h + 1) * block] = q_rows[i * block : (i + 1) * block]
            pair_rows[i, (2 * h + 1) * block : (2 * h + 2) * block] = do_rows[
                i * block : (i + 1) * block
            ]
    allowed = causal(block)

    def back(w):
        return w[:half], w[half:]

    for i in reversed(range(count)):
        start, stop = i * block, (i + 1) * block
        cos, sin = cos_ref[:, start:stop], sin_ref[:, start:stop]
        for h in range(heads):
            own = slice(h * HEAD_SIZE, (h + 1) * HEAD_SIZE)
            do = do_ref[own, start:stop]
            delta = jnp.sum(
                do.astype(jnp.float32) * o_ref[own, start:stop].astype(jnp.float32),
                axis=0, keepdims=True,
            )
            q_side = jnp.concatenate(
                [
                    q_ref[own, start:stop], penalty_ref[:, start:stop],
                    stacked_split(-lse_ref[0, h : h + 1, start:stop]), short[:, :block],
                ],
                axis=0,
            )
            do_side = jnp.concatenate([do, stacked_split(-delta), long[:, :block]], axis=0)
            left, middle, right = 2 * h * block, (2 * h + 1) * block, (2 * h + 2) * block
            probs = jnp.exp(
                jnp.where(allowed, product(key_rows[start:stop], q_side), masked_fill)
            )
            grads = (probs * product(value_rows[start:stop], do_side)).astype(jnp.bfloat16)
            weights[start:stop, left:middle] = grads
            weights[start:stop, middle:right] = probs.astype(jnp.bfloat16)
            dq = product(k_ref[:, start:stop], grads)
            if i:
                probs = jnp.exp(product(key_rows[:start], q_side))
                grads = (probs * product(value_rows[:start], do_side)).astype(jnp.bfloat16)
                weights[:start, left:middle] = grads
                weights[:start, middle:right] = probs.astype(jnp.bfloat16)
                dq = dq + product(k_ref[:, :start], grads)
            w1, w2 = back(dq * scale)
            dq_ref[h * HEAD_SIZE : h * HEAD_SIZE + half, start:stop] = (
                w1 * cos + w2 * sin
            ).astype(jnp.bfloat16)
            dq_ref[h * HEAD_SIZE + half : (h + 1) * HEAD_SIZE, start:stop] = (
                w2 * cos - w1 * sin
            ).astype(jnp.bfloat16)
        part = product(weights[:stop], pair_rows[i])
        if i == count - 1:
            sums[...] = part
        else:
            sums[:stop] = sums[:stop] + part
    both = sums[...].T
    w1, w2 = back(both[:HEAD_SIZE])
    cos, sin = cos_ref[...], sin_ref[...]
    dk_ref[:half] = (w1 * cos + w2 * sin).astype(jnp.bfloat16)
    dk_ref[half:] = (w2 * cos - w1 * sin).astype(jnp.bfloat16)
    dv_ref[...] = both[HEAD_SIZE:].astype(jnp.bfloat16)


def attention_specs(rows, low=0):
    group = QUERY_HEADS // KEY_VALUE_HEADS * HEAD_SIZE
    whole = pl.BlockSpec((SEGMENT_ROWS, rows), lambda g: (0, 0))
    table = pl.BlockSpec((HEAD_SIZE // 2, rows), lambda g: (0, 0))
    wide = pl.BlockSpec((group, rows), lambda g: (g + low, 0))
    narrow = pl.BlockSpec((HEAD_SIZE, rows), lambda g: (g + low, 0))
    lse = pl.BlockSpec((1, 8, rows), lambda g: (g + low, 0, 0))
    return whole, table, wide, narrow, lse


def attention_forward(onehot, penalty, q, k, v):
    rows = q.shape[1]
    whole, table, wide, narrow, lse = attention_specs(rows)
    return pl.pallas_call(
        attention_forward_kernel,
        grid=(KEY_VALUE_HEADS,),
        in_specs=[whole, whole, wide, narrow, narrow],
        out_specs=[wide, lse],
        out_shape=[
            jax.ShapeDtypeStruct(q.shape, jnp.bfloat16),
            jax.ShapeDtypeStruct((KEY_VALUE_HEADS, 8, rows), jnp.float32),
        ],
        scratch_shapes=[pltpu.VMEM((rows, 2 * HEAD_SIZE), jnp.bfloat16)],
        compiler_params=pltpu.CompilerParams(vmem_limit_bytes=32 << 20),
        cost_estimate=pl.CostEstimate(
            flops=8 * 1153 * 10**6 * 2, transcendentals=0, bytes_accessed=8 << 20
        ),
        name="attention_forward",
    )(onehot, penalty, q, k, v)


def attention_backward(onehot, penalty, cos, sin, q, k, v, o, do, lse_rows, low, count):
    rows = q.shape[1]
    block = min(QUERY_BLOCK, rows)
    heads = QUERY_HEADS // KEY_VALUE_HEADS
    whole, table, wide, narrow, lse = attention_specs(rows, low)
    _, _, wide_out, narrow_out, _ = attention_specs(rows)
    return pl.pallas_call(
        attention_backward_kernel,
        grid=(count,),
        in_specs=[whole, whole, table, table, wide, narrow, narrow, wide, wide, lse],
        out_specs=[wide_out, narrow_out, narrow_out],
        out_shape=[
            jax.ShapeDtypeStruct((count * size, rows), jnp.bfloat16)
            for size in (heads * HEAD_SIZE, HEAD_SIZE, HEAD_SIZE)
        ],
        scratch_shapes=[
            pltpu.VMEM((rows, 2 * HEAD_SIZE), jnp.bfloat16),
            pltpu.VMEM((rows, 2 * HEAD_SIZE), jnp.bfloat16),
            pltpu.VMEM((rows // block, 2 * heads * block, 2 * HEAD_SIZE), jnp.bfloat16),
            pltpu.VMEM((rows, 2 * heads * block), jnp.bfloat16),
            pltpu.VMEM((rows, 2 * HEAD_SIZE), jnp.float32),
        ],
        compiler_params=pltpu.CompilerParams(vmem_limit_bytes=40 << 20),
        cost_estimate=pl.CostEstimate(
            flops=count * 6 * 1153 * 10**6, transcendentals=0, bytes_accessed=count * 5 << 19
        ),
        name="attention_backward",
    )(onehot, penalty, cos, sin, q, k, v, o, do, lse_rows)


def product_nt(left, right):
    return lax.dot_general(
        left, right, (((1,), (1,)), ((), ())), preferred_element_type=jnp.float32
    )


def contract(left, right, left_dim, right_dim):
    return lax.dot_general(
        left, right, (((left_dim,), (right_dim,)), ((), ())), preferred_element_type=jnp.float32
    )


def assemble_kernel(cuts, place_ref, *refs):
    units, outs, sems = refs[:8], refs[8:-1], refs[-1]
    copies = []
    for unit in range(8):
        y = place_ref[0] ^ (unit >> 2)
        d = (place_ref[1] ^ ((unit >> 1) & 1)) * 2 + (place_ref[2] ^ (unit & 1))
        for at, (low, high) in enumerate(cuts):
            copies.append(
                pltpu.make_async_copy(
                    units[unit].at[:, low:high], outs[at].at[d, :, y], sems.at[unit, at]
                )
            )
    for copy in copies:
        copy.start()
    for copy in copies:
        copy.wait()


def assemble_unaligned(place, units, rows):
    whole = jnp.stack(units).reshape((2, 2, 2) + units[0].shape)
    for axis in range(3):
        whole = jnp.where(place[axis] == 0, whole, jnp.flip(whole, axis))
    whole = whole.transpose(1, 2, 3, 0, 4, 5)
    cuts = [sum(rows[:i]) for i in range(len(rows) + 1)]
    parts = [whole[:, :, :, :, low:high] for low, high in zip(cuts, cuts[1:])]
    return [part.reshape(4, -1, part.shape[-1]) for part in parts]


def assemble(place, units, rows):
    nz, total, width = units[0].shape
    if any(r % 8 for r in rows) or any(r % 16 for r in rows[:-1]):
        return assemble_unaligned(place, units, rows)
    cuts = [(sum(rows[:i]), sum(rows[: i + 1])) for i in range(len(rows))]
    outs = pl.pallas_call(
        functools.partial(assemble_kernel, cuts),
        grid_spec=pltpu.PrefetchScalarGridSpec(
            num_scalar_prefetch=1,
            grid=(1,),
            in_specs=[pl.BlockSpec(memory_space=pl.ANY)] * 8,
            out_specs=[pl.BlockSpec(memory_space=pl.ANY)] * len(cuts),
            scratch_shapes=[pltpu.SemaphoreType.DMA((8, len(cuts)))],
        ),
        out_shape=[jax.ShapeDtypeStruct((4, nz, 2, r, width), jnp.bfloat16) for r in rows],
        compiler_params=pltpu.CompilerParams(vmem_limit_bytes=4 << 20),
        cost_estimate=pl.CostEstimate(
            flops=0, transcendentals=0, bytes_accessed=2 * 8 * nz * total * width * 2
        ),
        name="assemble",
    )(place, *units)
    return [out.reshape(4, nz * 2 * r, width) for out, r in zip(outs, rows)]


def feed_forward_kernel(
    place_ref, n2_ref, gy_ref, down_ref, *refs
):
    units = refs[:-12]
    (mixed_ref, dn2_ref, gu_send_ref, gu_keep_ref, od_send_ref, od_keep_ref) = refs[-12:-6]
    pieces, weights, n2_across, grads, hidden, sems = refs[-6:]
    step = pl.program_id(0)
    rows, width = n2_ref.shape
    nz, unit_rows, double = units[0].shape
    ff = double // 2
    block = min(ROW_BLOCK, rows)

    def copies(at):
        xr, cr = 1 - at % 2, 1 - at // 2
        made = []
        if len(units) == 1:
            whole = units[0].at[(place_ref[1] ^ xr) * 2 + (place_ref[2] ^ cr)]
            return [pltpu.make_async_copy(whole, pieces.at[at, 0], sems.at[at, 0])]
        for yr in range(2):
            y = place_ref[0] ^ yr
            for z in range(nz):
                made.append(
                    pltpu.make_async_copy(
                        units[yr * 4 + xr * 2 + cr].at[z],
                        pieces.at[at, 2 * z + y],
                        sems.at[at, yr * nz + z],
                    )
                )
        return made

    @pl.when(step == 0)
    def _():
        for at in range(4):
            for copy in copies(at):
                copy.start()
        n2_across[...] = n2_ref[...].T
        mixed_ref[...] = jnp.zeros_like(mixed_ref)
        dn2_ref[...] = jnp.zeros_like(dn2_ref)

    for at in range(4):

        @pl.when(step == at)
        def _():
            for copy in copies(at):
                copy.wait()

    for f in range(pieces.shape[1]):
        weights[f * pieces.shape[2] : (f + 1) * pieces.shape[2]] = pieces[step, f]

    def chunk(i, carry):
        part = pl.ds(pl.multiple_of(i * block, block), block)
        n2 = n2_ref[part]
        gate = product(n2, weights[:, :ff])
        up = product(n2, weights[:, ff:])
        sigma = jax.nn.sigmoid(gate)
        silu = gate * sigma
        hid = (silu * up).astype(jnp.bfloat16)
        hidden[part] = hid
        dhid = product_nt(gy_ref[0, part], down_ref[0])
        for d in range(1, 4):
            dhid = dhid + product_nt(gy_ref[d, part], down_ref[d])
        grads[part, :ff] = (dhid * up * (sigma * (1.0 + gate * (1.0 - sigma)))).astype(
            jnp.bfloat16
        )
        grads[part, ff:] = (dhid * silu).astype(jnp.bfloat16)
        for d in range(4):
            mixed_ref[d, part] = mixed_ref[d, part] + product(hid, down_ref[d])
        dn2_ref[part] = dn2_ref[part] + product_nt(grads[part], weights[...])
        return carry

    lax.fori_loop(0, rows // block, chunk, 0)

    def weight_grads(out_ref):
        for low in range(0, double, 256):
            out_ref[0, :, low : low + 256] = product(
                n2_across[...], grads[:, low : low + 256]
            ).astype(jnp.bfloat16)

    @pl.when(step < 2)
    def _():
        weight_grads(gu_send_ref)

    @pl.when(step >= 2)
    def _():
        weight_grads(gu_keep_ref)

    hidden_across = hidden[...].T
    own = od_send_ref.shape[1]
    depth = ff // own
    for cr, out_ref in ((1, od_send_ref), (0, od_keep_ref)):
        for k in range(2):
            d = (place_ref[1] ^ (1 - k)) * 2 + (place_ref[2] ^ cr)
            value = product(hidden_across, gy_ref[d]).astype(jnp.bfloat16)
            for f in range(own):
                out_ref[k, f, :depth] = value[f * depth : (f + 1) * depth]


def feed_forward(place, n2, gy, down, units, od_rows):
    rows, width = n2.shape
    fsdp, depth = 2 * units[0].shape[0], units[0].shape[1]
    if depth % 8:
        units = assemble(place, units, [depth])
        depth = width
    double = units[0].shape[2]
    ff = double // 2
    d_cols = gy.shape[2]
    own = fsdp // 4

    def hidden_block(s, place_ref):
        return (place_ref[1] ^ (1 - s % 2)) * 2 + (place_ref[2] ^ (1 - s // 2))

    once = pl.Buffered(1)
    flops = 2 * rows * width * 4 * ff * 9
    return pl.pallas_call(
        feed_forward_kernel,
        grid_spec=pltpu.PrefetchScalarGridSpec(
            num_scalar_prefetch=1,
            grid=(4,),
            in_specs=[
                pl.BlockSpec((rows, width), lambda s, p: (0, 0), pipeline_mode=once),
                pl.BlockSpec((4, rows, d_cols), lambda s, p: (0, 0, 0), pipeline_mode=once),
                pl.BlockSpec((4, ff, d_cols), lambda s, p: (0, hidden_block(s, p), 0)),
            ]
            + [pl.BlockSpec(memory_space=pl.ANY)] * len(units),
            out_specs=[
                pl.BlockSpec((4, rows, d_cols), lambda s, p: (0, 0, 0), pipeline_mode=once),
                pl.BlockSpec((rows, width), lambda s, p: (0, 0), pipeline_mode=once),
                pl.BlockSpec((1, width, double), lambda s, p: (jnp.minimum(s, 1), 0, 0)),
                pl.BlockSpec((1, width, double), lambda s, p: (jnp.maximum(s - 2, 0), 0, 0)),
                pl.BlockSpec((2, own, od_rows, d_cols), lambda s, p: (0, hidden_block(s, p), 0, 0)),
                pl.BlockSpec((2, own, od_rows, d_cols), lambda s, p: (0, hidden_block(s, p), 0, 0)),
            ],
            scratch_shapes=[
                pltpu.VMEM((4, width // depth, depth, double), jnp.bfloat16),
                pltpu.VMEM((width, double), jnp.bfloat16),
                pltpu.VMEM((width, rows), jnp.bfloat16),
                pltpu.VMEM((rows, double), jnp.bfloat16),
                pltpu.VMEM((rows, ff), jnp.bfloat16),
                pltpu.SemaphoreType.DMA((4, fsdp)),
            ],
        ),
        out_shape=[
            jax.ShapeDtypeStruct((4, rows, d_cols), jnp.float32),
            jax.ShapeDtypeStruct((rows, width), jnp.float32),
            jax.ShapeDtypeStruct((2, width, double), jnp.bfloat16),
            jax.ShapeDtypeStruct((2, width, double), jnp.bfloat16),
            jax.ShapeDtypeStruct((2, fsdp, od_rows, d_cols), jnp.bfloat16),
            jax.ShapeDtypeStruct((2, fsdp, od_rows, d_cols), jnp.bfloat16),
        ],
        compiler_params=pltpu.CompilerParams(vmem_limit_bytes=60 << 20),
        cost_estimate=pl.CostEstimate(flops=flops, transcendentals=0, bytes_accessed=48 << 20),
        name="feed_forward",
    )(place, n2, gy, down, *units)


def after(value, *others):
    return lax.optimization_barrier((value, *others))[0]


def swap(value, axes):
    count = 2 ** len(axes)
    return lax.ppermute(value, axes, [(i, count - 1 - i) for i in range(count)])


def z_partner(value, mask, nz):
    return lax.ppermute(value, "z", [(i, i ^ mask) for i in range(nz)])


def gather_z(shard, nz, *before):
    if nz != 4:
        return lax.all_gather(shard, "z", axis=0, tiled=False)
    me = lax.axis_index("z")
    unit = jnp.zeros((nz,) + shard.shape, shard.dtype)
    pieces = [z_partner(shard, mask, nz) if mask else shard for mask in range(nz)]
    if before:
        pieces = lax.optimization_barrier((*pieces, *before))[:nz]
    for mask, piece in enumerate(pieces):
        unit = lax.dynamic_update_slice(unit, piece[None], (me ^ mask,) + (0,) * shard.ndim)
    return unit


def scatter_z(unit, nz):
    if nz != 4:
        return lax.psum_scatter(unit, "z", scatter_dimension=0, tiled=False).astype(jnp.float32)
    me = lax.axis_index("z")

    def part(mask):
        return lax.dynamic_index_in_dim(unit, me ^ mask, 0, keepdims=False)

    total = part(0).astype(jnp.float32)
    for mask in range(1, nz):
        total = total + z_partner(part(mask), mask, nz).astype(jnp.float32)
    return total


def units_of(own, along_y, along_x, along_both):
    four = (own, along_x, along_y, along_both)
    across = [swap(unit, ("c",)) for unit in four]
    order = []
    for yr in range(2):
        for xr in range(2):
            order += [four[yr * 2 + xr], across[yr * 2 + xr]]
    return order


def norm_back(values, scale_rows, gain_wide, upstream):
    weighted = gain_wide[None, :] * upstream
    return scale_rows * weighted - values * scale_rows**3 * jnp.mean(
        weighted * values, axis=1, keepdims=True
    )


def norm_scale(values):
    return lax.rsqrt(jnp.mean(values * values, axis=1, keepdims=True) + epsilon)


def shards(
    tokens,
    seq_lengths,
    norm1_gain,
    q_weight,
    k_weight,
    v_weight,
    o_weight,
    norm2_gain,
    gate_weight,
    up_weight,
    down_weight,
    cotangent,
):
    f32, bf16 = jnp.float32, jnp.bfloat16
    rows, width = tokens.shape
    nz = lax.axis_size("z")
    me_z, me_y, me_x, me_c = (lax.axis_index(a) for a in ("z", "y", "x", "c"))
    place = jnp.stack([me_y, me_x, me_c]).astype(jnp.int32)
    r_in, q_cols = q_weight.shape
    k_cols = k_weight.shape[1]
    qkv = q_cols + 2 * k_cols
    lanes = -(-(qkv + 2) // 128) * 128
    down_rows = down_weight.shape[0]
    o_rows = o_weight.shape[0]
    ff = gate_weight.shape[1]

    pack_a = jnp.concatenate(
        [
            q_weight,
            k_weight,
            v_weight,
            norm1_gain[:, None],
            norm2_gain[:, None],
            jnp.zeros((r_in, lanes - qkv - 2), bf16),
        ],
        axis=1,
    )
    filler = -(down_rows + o_rows) % 16
    pack_od = jnp.pad(jnp.concatenate([down_weight, o_weight], axis=0), ((0, filler), (0, 0)))
    pack_gu = jnp.concatenate([gate_weight, up_weight], axis=1)
    unit_a = gather_z(pack_a, nz)
    around = [swap(unit_a, axes) for axes in (("y",), ("x",), ("y", "x"))]
    units_a = units_of(unit_a, *around)
    [weights_a] = assemble(place, units_a, [r_in])
    unit_od = gather_z(after(pack_od, *units_a), nz)
    unit_gu = gather_z(after(pack_gu, unit_a), nz, *around)
    od_y, od_x = swap(unit_od, ("y",)), swap(unit_od, ("x",))
    gu_y, gu_x = swap(unit_gu, ("y",)), swap(unit_gu, ("x",))
    gain_one = weights_a[0, :, qkv].astype(f32)
    gain_two = weights_a[0, :, qkv + 1].astype(f32)

    lengths = seq_lengths[0]
    slots = jnp.arange(lengths.shape[0])
    ends = jnp.sum(jnp.where(slots[None, :] <= slots[:, None], lengths[None, :], 0), axis=1)
    places = jnp.arange(rows, dtype=jnp.int32)
    passed = (places[None, :] >= ends[:, None]).astype(jnp.int32)
    segment = jnp.sum(passed, axis=0)
    position = places - jnp.sum(passed * lengths[:, None], axis=0)
    live = (places < ends[-1]).astype(f32)
    same = jnp.arange(SEGMENT_ROWS)[:, None] == segment[None, :]
    onehot = same.astype(bf16)
    penalty = jnp.where(same, 0.0, masked_fill).astype(bf16)
    half = HEAD_SIZE // 2
    inverse = jnp.exp(
        -math.log(rope_base) * (jnp.arange(half, dtype=f32) * (2.0 / HEAD_SIZE))
    )
    angle = inverse[:, None] * position.astype(f32)[None, :]
    cos, sin = jnp.cos(angle), jnp.sin(angle)

    x = tokens.astype(f32)
    scale_one = norm_scale(x)
    n1 = (x * scale_one * gain_one[None, :]).astype(bf16)
    proj = lax.dot_general(
        weights_a, n1, (((1,), (1,)), ((), ())), preferred_element_type=f32
    )
    q_across = proj[:, :q_cols].reshape(QUERY_HEADS, 2, half, rows)
    k_across = proj[:, q_cols : q_cols + k_cols].reshape(KEY_VALUE_HEADS, 2, half, rows)
    v_across = proj[:, q_cols + k_cols : qkv].reshape(-1, rows).astype(bf16)

    def rope(u):
        u1, u2 = u[:, 0], u[:, 1]
        return (
            jnp.stack([u1 * cos - u2 * sin, u2 * cos + u1 * sin], axis=1)
            .astype(bf16)
            .reshape(-1, rows)
        )

    qr = rope(q_across) * jnp.asarray(1.0 / math.sqrt(HEAD_SIZE), bf16)
    kr = rope(k_across)
    qr = after(qr, unit_od, unit_gu)
    att, lse = attention_forward(onehot, penalty, qr, kr, v_across)
    od_y, od_x, gu_y, gu_x = (after(a, att) for a in (od_y, od_x, gu_y, gu_x))
    units_od = units_of(unit_od, od_y, od_x, swap(od_y, ("x",)))
    units_gu = units_of(unit_gu, gu_y, gu_x, swap(gu_x, ("y",)))
    down_all, o_all = assemble(place, units_od, [down_rows, o_rows + filler])
    o_all = o_all.reshape(4, 2 * nz, o_rows + filler, -1)[:, :, :o_rows].reshape(4, width, -1)
    o_full = jnp.concatenate([o_all[d] for d in range(4)], axis=1)
    hmid = x + contract(att, o_full, 0, 0)

    scale_two = norm_scale(hmid)
    n2 = (hmid * scale_two * gain_two[None, :]).astype(bf16)
    gy = live[:, None] * cotangent.astype(f32)
    d_cols = width // 4
    gy_low = gy.astype(bf16)
    gy_parts = jnp.stack([gy_low[:, d * d_cols : (d + 1) * d_cols] for d in range(4)])
    mixed_parts, dn2, gu_send, gu_keep, od_send, od_keep = feed_forward(
        place, n2, gy_parts, down_all, units_gu, down_rows + o_rows + filler
    )
    dh = gy + norm_back(hmid, scale_two, gain_two, dn2)
    da = dh.astype(bf16)

    def quarter(halves, k, y):
        part = lax.dynamic_slice(halves, (k, 0, y, 0, 0), (1, nz, 1) + halves.shape[3:])
        return part.reshape((nz,) + halves.shape[3:])

    gu_shape = (2, nz, 2, r_in, 2 * ff)
    gu_keep = gu_keep.reshape(gu_shape)
    gu_got = after(swap(gu_send, ("c",)), da).reshape(gu_shape)

    def both_gu(k, y):
        return quarter(gu_keep, k, y) + quarter(gu_got, k, y)

    gu_first = both_gu(0, 1 - me_y)
    gu_first_got = swap(gu_first, ("y",))

    da = after(da, gu_first)
    da_parts = jnp.stack([da[:, d * d_cols : (d + 1) * d_cols] for d in range(4)])
    grad_o = lax.dot_general(
        att, da_parts, (((1,), (1,)), ((), ())), preferred_element_type=f32
    )
    grad_o = grad_o.astype(bf16).transpose(1, 0, 2).reshape(2, 2, 2 * nz, o_rows, d_cols)
    datt = contract(o_full, da, 1, 1).astype(bf16)

    def with_o(parts, c):
        own = lax.dynamic_index_in_dim(grad_o, c, 1, keepdims=False)
        own = jnp.stack(
            [
                lax.dynamic_index_in_dim(own, 1 - me_x, 0, keepdims=False),
                lax.dynamic_index_in_dim(own, me_x, 0, keepdims=False),
            ]
        )
        return lax.dynamic_update_slice(parts, own, (0, 0, down_rows, 0))

    od_shape = (2, nz, 2, down_rows + o_rows + filler, d_cols)
    od_send = with_o(od_send, 1 - me_c)
    od_got = swap(od_send, ("c",)).reshape(od_shape)
    od_keep = with_o(od_keep, me_c).reshape(od_shape)

    def both_od(k, y):
        return quarter(od_keep, k, y) + quarter(od_got, k, y)

    od_first = both_od(0, 1 - me_y)
    od_first_got = swap(od_first, ("x",))

    back = functools.partial(attention_backward, onehot, penalty, cos, sin, qr, kr, v_across, att)
    first = back(after(datt, gu_first, od_first), lse, 0, 2)
    gu_x = both_gu(0, me_y) + after(gu_first_got, first[0])
    gu_second = both_gu(1, 1 - me_y)
    gu_x_got, gu_second_got = swap(gu_x, ("x",)), swap(gu_second, ("y",))
    second = back(after(datt, gu_x, gu_second, first[0]), lse, 2, 2)
    od_y = both_od(1, 1 - me_y) + after(od_first_got, second[0])
    od_second = both_od(0, me_y)
    od_y_got, od_second_got = swap(od_y, ("y",)), swap(od_second, ("x",))
    third = back(after(datt, od_y, od_second, second[0]), lse, 4, 1)
    dq, dk, dv = (jnp.concatenate(group) for group in zip(first, second, third))
    dproj = jnp.concatenate(
        [
            dq.reshape(4, q_cols, rows),
            dk.reshape(4, k_cols, rows),
            dv.reshape(4, k_cols, rows),
            jnp.zeros((4, lanes - qkv, rows), bf16),
        ],
        axis=1,
    )
    grad_a = lax.dot_general(dproj, n1, (((2,), (0,)), ((), ())), preferred_element_type=f32)
    grad_a = grad_a.transpose(0, 2, 1).astype(bf16).reshape(2, 2, nz, 2, r_in, lanes)
    a_send = lax.dynamic_index_in_dim(grad_a, 1 - me_c, 1, keepdims=False)
    a_keep = lax.dynamic_index_in_dim(grad_a, me_c, 1, keepdims=False)
    dn1 = lax.dot_general(
        after(dproj, a_send), weights_a, (((0, 1), (0, 2)), ((), ())), preferred_element_type=f32
    )
    grad_gain_two = jnp.sum(after(dn2, dn1) * hmid * scale_two, axis=0)
    gains = jnp.stack([jnp.sum(dn1 * x * scale_one, axis=0), grad_gain_two], axis=1)
    gains = (gains + swap(gains.astype(bf16), ("c",)).astype(f32)).astype(bf16)
    gains = jnp.pad(gains, ((0, 0), (qkv, lanes - qkv - 2)))
    gains = gains.reshape(1, nz, 2, r_in, lanes)
    a_sum = a_keep + swap(a_send, ("c",)) + gains
    def part_a(x, y):
        return lax.dynamic_index_in_dim(
            lax.dynamic_index_in_dim(a_sum, x, 0, keepdims=False), y, 1, keepdims=False
        )

    a_sends = [part_a(1 - me_x, me_y), part_a(me_x, 1 - me_y), part_a(1 - me_x, 1 - me_y)]
    a_got = [swap(part, axes) for part, axes in zip(a_sends, (("x",), ("y",), ("y", "x")))]
    gu_unit = both_gu(1, me_y) + after(gu_second_got, *a_sends) + after(gu_x_got, *a_sends)
    sum_gu = scatter_z(gu_unit, nz)
    od_unit = both_od(1, me_y) + after(od_second_got, gu_unit) + after(od_y_got, gu_unit)
    sum_od = scatter_z(od_unit, nz)
    a_got = [after(got, od_unit) for got in a_got]
    a_unit = part_a(me_x, me_y) + a_got[0] + a_got[1] + a_got[2]
    sum_a = scatter_z(a_unit, nz)
    mixed_late = after(mixed_parts, *a_sends)
    mixed = (
        live[:, None] * (hmid + jnp.concatenate([mixed_late[d] for d in range(4)], axis=1))
    ).astype(bf16)
    grad_tokens = dh + norm_back(x, scale_one, gain_one, after(dn1, *a_sends))
    return (
        mixed,
        grad_tokens,
        sum_a[:, qkv],
        sum_a[:, :q_cols],
        sum_a[:, q_cols : q_cols + k_cols],
        sum_a[:, q_cols + k_cols : qkv],
        sum_od[down_rows : down_rows + o_rows],
        sum_a[:, qkv + 1],
        sum_gu[:, :ff],
        sum_gu[:, ff:],
        sum_od[:down_rows],
    )


def solution(mesh):
    fsdp, dp = mesh.devices.shape
    assert dp == 4 and fsdp % 2 == 0
    split = Mesh(mesh.devices.reshape(fsdp // 2, 2, 2, 2), ("z", "y", "x", "c"))
    rows, grid, gain = P(("z", "y", "x", "c"), None), P(("z", "y"), ("x", "c")), P(("z", "y"))
    return jax.shard_map(
        shards,
        mesh=split,
        in_specs=(rows, rows, gain, grid, grid, grid, grid, gain, grid, grid, grid, rows),
        out_specs=(rows, rows, gain, grid, grid, grid, grid, gain, grid, grid, grid),
        check_vma=False,
    )
```

```python
import functools
import math
import jax
import jax.numpy as jnp
from jax import lax
from jax.experimental import pallas as pl
from jax.experimental.pallas import tpu as pltpu
from jax.sharding import Mesh
from jax.sharding import PartitionSpec as P

QUERY_HEADS = 15
KEY_VALUE_HEADS = 5
HEAD_SIZE = 64
QUERY_BLOCK = 256
ROW_BLOCK = 512
SEGMENT_ROWS = 16
epsilon = 1e-05
rope_base = 100000.0
masked_fill = -1e30


def product(left, right):
    return jnp.dot(left, right, preferred_element_type=jnp.float32)


def stacked_split(row):
    high = row.astype(jnp.bfloat16).astype(jnp.float32)
    middle = (row - high).astype(jnp.bfloat16).astype(jnp.float32)
    low = row - high - middle
    place = lax.broadcasted_iota(jnp.int32, (SEGMENT_ROWS, row.shape[1]), 0)
    return jnp.where(
        place == 0, high, jnp.where(place == 1, middle, jnp.where(place == 2, low, 0.0))
    ).astype(jnp.bfloat16)


def causal(block):
    key_place = lax.broadcasted_iota(jnp.int32, (block, block), 0)
    query_place = lax.broadcasted_iota(jnp.int32, (block, block), 1)
    return key_place <= query_place


def attention_forward_kernel(onehot_ref, penalty_ref, q_ref, k_ref, v_ref, o_ref, lse_ref, key_rows):
    rows = q_ref.shape[1]
    block = min(QUERY_BLOCK, rows)
    filler = jnp.zeros((HEAD_SIZE - SEGMENT_ROWS, rows), jnp.bfloat16)
    key_rows[...] = jnp.concatenate([k_ref[...], onehot_ref[...], filler], axis=0).T
    allowed = causal(block)
    lse_ref[...] = jnp.zeros_like(lse_ref)
    for i in range(rows // block):
        start, stop = i * block, (i + 1) * block
        for h in range(q_ref.shape[0] // HEAD_SIZE):
            q_side = jnp.concatenate(
                [
                    q_ref[h * HEAD_SIZE : (h + 1) * HEAD_SIZE, start:stop],
                    penalty_ref[:, start:stop],
                    filler[:, :block],
                ],
                axis=0,
            )
            near = jnp.where(allowed, product(key_rows[start:stop], q_side), masked_fill)
            peak = jnp.max(near, axis=0, keepdims=True)
            if i:
                far = product(key_rows[:start], q_side)
                peak = jnp.maximum(peak, jnp.max(far, axis=0, keepdims=True))
            near = jnp.exp(near - peak)
            total = jnp.sum(near, axis=0, keepdims=True)
            out = product(v_ref[:, start:stop], near.astype(jnp.bfloat16))
            if i:
                far = jnp.exp(far - peak)
                total = total + jnp.sum(far, axis=0, keepdims=True)
                out = out + product(v_ref[:, :start], far.astype(jnp.bfloat16))
            o_ref[h * HEAD_SIZE : (h + 1) * HEAD_SIZE, start:stop] = (out / total).astype(
                jnp.bfloat16
            )
            lse_ref[0, h : h + 1, start:stop] = peak + jnp.log(total)


def attention_backward_kernel(
    onehot_ref, penalty_ref, cos_ref, sin_ref, q_ref, k_ref, v_ref, o_ref, do_ref, lse_ref,
    dq_ref, dk_ref, dv_ref, key_rows, value_rows, pair_rows, weights, sums,
):
    rows = q_ref.shape[1]
    block = min(QUERY_BLOCK, rows)
    heads = q_ref.shape[0] // HEAD_SIZE
    half = HEAD_SIZE // 2
    scale = 1.0 / math.sqrt(HEAD_SIZE)
    ones = jnp.ones((SEGMENT_ROWS, rows), jnp.bfloat16)
    zeros = jnp.zeros((HEAD_SIZE, rows), jnp.bfloat16)
    short = zeros[: HEAD_SIZE - 2 * SEGMENT_ROWS]
    long = zeros[: HEAD_SIZE - SEGMENT_ROWS]
    key_rows[...] = jnp.concatenate([k_ref[...], onehot_ref[...], ones, short], axis=0).T
    value_rows[...] = jnp.concatenate([v_ref[...], ones, long], axis=0).T
    count = rows // block
    for h in range(heads):
        q_rows = jnp.concatenate([q_ref[h * HEAD_SIZE : (h + 1) * HEAD_SIZE], zeros], axis=0).T
        do_rows = jnp.concatenate([zeros, do_ref[h * HEAD_SIZE : (h + 1) * HEAD_SIZE]], axis=0).T
        for i in range(count):
            pair_rows[i, 2 * h * block : (2 * h + 1) * block] = q_rows[i * block : (i + 1) * block]
            pair_rows[i, (2 * h + 1) * block : (2 * h + 2) * block] = do_rows[
                i * block : (i + 1) * block
            ]
    allowed = causal(block)

    def back(w):
        return w[:half], w[half:]

    for i in reversed(range(count)):
        start, stop = i * block, (i + 1) * block
        cos, sin = cos_ref[:, start:stop], sin_ref[:, start:stop]
        for h in range(heads):
            own = slice(h * HEAD_SIZE, (h + 1) * HEAD_SIZE)
            do = do_ref[own, start:stop]
            delta = jnp.sum(
                do.astype(jnp.float32) * o_ref[own, start:stop].astype(jnp.float32),
                axis=0, keepdims=True,
            )
            q_side = jnp.concatenate(
                [
                    q_ref[own, start:stop], penalty_ref[:, start:stop],
                    stacked_split(-lse_ref[0, h : h + 1, start:stop]), short[:, :block],
                ],
                axis=0,
            )
            do_side = jnp.concatenate([do, stacked_split(-delta), long[:, :block]], axis=0)
            left, middle, right = 2 * h * block, (2 * h + 1) * block, (2 * h + 2) * block
            probs = jnp.exp(
                jnp.where(allowed, product(key_rows[start:stop], q_side), masked_fill)
            )
            grads = (probs * product(value_rows[start:stop], do_side)).astype(jnp.bfloat16)
            weights[start:stop, left:middle] = grads
            weights[start:stop, middle:right] = probs.astype(jnp.bfloat16)
            dq = product(k_ref[:, start:stop], grads)
            if i:
                probs = jnp.exp(product(key_rows[:start], q_side))
                grads = (probs * product(value_rows[:start], do_side)).astype(jnp.bfloat16)
                weights[:start, left:middle] = grads
                weights[:start, middle:right] = probs.astype(jnp.bfloat16)
                dq = dq + product(k_ref[:, :start], grads)
            w1, w2 = back(dq * scale)
            dq_ref[h * HEAD_SIZE : h * HEAD_SIZE + half, start:stop] = (
                w1 * cos + w2 * sin
            ).astype(jnp.bfloat16)
            dq_ref[h * HEAD_SIZE + half : (h + 1) * HEAD_SIZE, start:stop] = (
                w2 * cos - w1 * sin
            ).astype(jnp.bfloat16)
        part = product(weights[:stop], pair_rows[i])
        if i == count - 1:
            sums[...] = part
        else:
            sums[:stop] = sums[:stop] + part
    both = sums[...].T
    w1, w2 = back(both[:HEAD_SIZE])
    cos, sin = cos_ref[...], sin_ref[...]
    dk_ref[:half] = (w1 * cos + w2 * sin).astype(jnp.bfloat16)
    dk_ref[half:] = (w2 * cos - w1 * sin).astype(jnp.bfloat16)
    dv_ref[...] = both[HEAD_SIZE:].astype(jnp.bfloat16)


def attention_specs(rows, low=0):
    group = QUERY_HEADS // KEY_VALUE_HEADS * HEAD_SIZE
    whole = pl.BlockSpec((SEGMENT_ROWS, rows), lambda g: (0, 0))
    table = pl.BlockSpec((HEAD_SIZE // 2, rows), lambda g: (0, 0))
    wide = pl.BlockSpec((group, rows), lambda g: (g + low, 0))
    narrow = pl.BlockSpec((HEAD_SIZE, rows), lambda g: (g + low, 0))
    lse = pl.BlockSpec((1, 8, rows), lambda g: (g + low, 0, 0))
    return whole, table, wide, narrow, lse


def attention_forward(onehot, penalty, q, k, v):
    rows = q.shape[1]
    whole, table, wide, narrow, lse = attention_specs(rows)
    return pl.pallas_call(
        attention_forward_kernel,
        grid=(KEY_VALUE_HEADS,),
        in_specs=[whole, whole, wide, narrow, narrow],
        out_specs=[wide, lse],
        out_shape=[
            jax.ShapeDtypeStruct(q.shape, jnp.bfloat16),
            jax.ShapeDtypeStruct((KEY_VALUE_HEADS, 8, rows), jnp.float32),
        ],
        scratch_shapes=[pltpu.VMEM((rows, 2 * HEAD_SIZE), jnp.bfloat16)],
        compiler_params=pltpu.CompilerParams(vmem_limit_bytes=32 << 20),
        cost_estimate=pl.CostEstimate(
            flops=8 * 1153 * 10**6 * 2, transcendentals=0, bytes_accessed=8 << 20
        ),
        name="attention_forward",
    )(onehot, penalty, q, k, v)


def attention_backward(onehot, penalty, cos, sin, q, k, v, o, do, lse_rows, low, count):
    rows = q.shape[1]
    block = min(QUERY_BLOCK, rows)
    heads = QUERY_HEADS // KEY_VALUE_HEADS
    whole, table, wide, narrow, lse = attention_specs(rows, low)
    _, _, wide_out, narrow_out, _ = attention_specs(rows)
    return pl.pallas_call(
        attention_backward_kernel,
        grid=(count,),
        in_specs=[whole, whole, table, table, wide, narrow, narrow, wide, wide, lse],
        out_specs=[wide_out, narrow_out, narrow_out],
        out_shape=[
            jax.ShapeDtypeStruct((count * size, rows), jnp.bfloat16)
            for size in (heads * HEAD_SIZE, HEAD_SIZE, HEAD_SIZE)
        ],
        scratch_shapes=[
            pltpu.VMEM((rows, 2 * HEAD_SIZE), jnp.bfloat16),
            pltpu.VMEM((rows, 2 * HEAD_SIZE), jnp.bfloat16),
            pltpu.VMEM((rows // block, 2 * heads * block, 2 * HEAD_SIZE), jnp.bfloat16),
            pltpu.VMEM((rows, 2 * heads * block), jnp.bfloat16),
            pltpu.VMEM((rows, 2 * HEAD_SIZE), jnp.float32),
        ],
        compiler_params=pltpu.CompilerParams(vmem_limit_bytes=40 << 20),
        cost_estimate=pl.CostEstimate(
            flops=count * 6 * 1153 * 10**6, transcendentals=0, bytes_accessed=count * 5 << 19
        ),
        name="attention_backward",
    )(onehot, penalty, cos, sin, q, k, v, o, do, lse_rows)


def product_nt(left, right):
    return lax.dot_general(
        left, right, (((1,), (1,)), ((), ())), preferred_element_type=jnp.float32
    )


def contract(left, right, left_dim, right_dim):
    return lax.dot_general(
        left, right, (((left_dim,), (right_dim,)), ((), ())), preferred_element_type=jnp.float32
    )


def assemble_kernel(cuts, place_ref, *refs):
    units, outs, sems = refs[:8], refs[8:-1], refs[-1]
    copies = []
    for unit in range(8):
        y = place_ref[0] ^ (unit >> 2)
        d = (place_ref[1] ^ ((unit >> 1) & 1)) * 2 + (place_ref[2] ^ (unit & 1))
        for at, (low, high) in enumerate(cuts):
            copies.append(
                pltpu.make_async_copy(
                    units[unit].at[:, low:high], outs[at].at[d, :, y], sems.at[unit, at]
                )
            )
    for copy in copies:
        copy.start()
    for copy in copies:
        copy.wait()


def assemble_unaligned(place, units, rows):
    whole = jnp.stack(units).reshape((2, 2, 2) + units[0].shape)
    for axis in range(3):
        whole = jnp.where(place[axis] == 0, whole, jnp.flip(whole, axis))
    whole = whole.transpose(1, 2, 3, 0, 4, 5)
    cuts = [sum(rows[:i]) for i in range(len(rows) + 1)]
    parts = [whole[:, :, :, :, low:high] for low, high in zip(cuts, cuts[1:])]
    return [part.reshape(4, -1, part.shape[-1]) for part in parts]


def assemble(place, units, rows):
    nz, total, width = units[0].shape
    if any(r % 8 for r in rows) or any(r % 16 for r in rows[:-1]):
        return assemble_unaligned(place, units, rows)
    cuts = [(sum(rows[:i]), sum(rows[: i + 1])) for i in range(len(rows))]
    outs = pl.pallas_call(
        functools.partial(assemble_kernel, cuts),
        grid_spec=pltpu.PrefetchScalarGridSpec(
            num_scalar_prefetch=1,
            grid=(1,),
            in_specs=[pl.BlockSpec(memory_space=pl.ANY)] * 8,
            out_specs=[pl.BlockSpec(memory_space=pl.ANY)] * len(cuts),
            scratch_shapes=[pltpu.SemaphoreType.DMA((8, len(cuts)))],
        ),
        out_shape=[jax.ShapeDtypeStruct((4, nz, 2, r, width), jnp.bfloat16) for r in rows],
        compiler_params=pltpu.CompilerParams(vmem_limit_bytes=4 << 20),
        cost_estimate=pl.CostEstimate(
            flops=0, transcendentals=0, bytes_accessed=2 * 8 * nz * total * width * 2
        ),
        name="assemble",
    )(place, *units)
    return [out.reshape(4, nz * 2 * r, width) for out, r in zip(outs, rows)]


def feed_forward_kernel(
    place_ref, n2_ref, gy_ref, down_ref, *refs
):
    units = refs[:-12]
    (mixed_ref, dn2_ref, gu_send_ref, gu_keep_ref, od_send_ref, od_keep_ref) = refs[-12:-6]
    pieces, weights, n2_across, grads, hidden, sems = refs[-6:]
    step = pl.program_id(0)
    rows, width = n2_ref.shape
    nz, unit_rows, double = units[0].shape
    ff = double // 2
    block = min(ROW_BLOCK, rows)

    def copies(at):
        xr, cr = 1 - at % 2, 1 - at // 2
        made = []
        if len(units) == 1:
            whole = units[0].at[(place_ref[1] ^ xr) * 2 + (place_ref[2] ^ cr)]
            return [pltpu.make_async_copy(whole, pieces.at[at, 0], sems.at[at, 0])]
        for yr in range(2):
            y = place_ref[0] ^ yr
            for z in range(nz):
                made.append(
                    pltpu.make_async_copy(
                        units[yr * 4 + xr * 2 + cr].at[z],
                        pieces.at[at, 2 * z + y],
                        sems.at[at, yr * nz + z],
                    )
                )
        return made

    @pl.when(step == 0)
    def _():
        for at in range(4):
            for copy in copies(at):
                copy.start()
        n2_across[...] = n2_ref[...].T
        mixed_ref[...] = jnp.zeros_like(mixed_ref)
        dn2_ref[...] = jnp.zeros_like(dn2_ref)

    for at in range(4):

        @pl.when(step == at)
        def _():
            for copy in copies(at):
                copy.wait()

    for f in range(pieces.shape[1]):
        weights[f * pieces.shape[2] : (f + 1) * pieces.shape[2]] = pieces[step, f]

    def chunk(i, carry):
        part = pl.ds(pl.multiple_of(i * block, block), block)
        n2 = n2_ref[part]
        gate = product(n2, weights[:, :ff])
        up = product(n2, weights[:, ff:])
        sigma = jax.nn.sigmoid(gate)
        silu = gate * sigma
        hid = (silu * up).astype(jnp.bfloat16)
        hidden[part] = hid
        dhid = product_nt(gy_ref[0, part], down_ref[0])
        for d in range(1, 4):
            dhid = dhid + product_nt(gy_ref[d, part], down_ref[d])
        grads[part, :ff] = (dhid * up * (sigma * (1.0 + gate * (1.0 - sigma)))).astype(
            jnp.bfloat16
        )
        grads[part, ff:] = (dhid * silu).astype(jnp.bfloat16)
        for d in range(4):
            mixed_ref[d, part] = mixed_ref[d, part] + product(hid, down_ref[d])
        dn2_ref[part] = dn2_ref[part] + product_nt(grads[part], weights[...])
        return carry

    lax.fori_loop(0, rows // block, chunk, 0)

    def weight_grads(out_ref):
        for low in range(0, double, 256):
            out_ref[0, :, low : low + 256] = product(
                n2_across[...], grads[:, low : low + 256]
            ).astype(jnp.bfloat16)

    @pl.when(step < 2)
    def _():
        weight_grads(gu_send_ref)

    @pl.when(step >= 2)
    def _():
        weight_grads(gu_keep_ref)

    hidden_across = hidden[...].T
    own = od_send_ref.shape[1]
    depth = ff // own
    for cr, out_ref in ((1, od_send_ref), (0, od_keep_ref)):
        for k in range(2):
            d = (place_ref[1] ^ (1 - k)) * 2 + (place_ref[2] ^ cr)
            value = product(hidden_across, gy_ref[d]).astype(jnp.bfloat16)
            for f in range(own):
                out_ref[k, f, :depth] = value[f * depth : (f + 1) * depth]


def feed_forward(place, n2, gy, down, units, od_rows):
    rows, width = n2.shape
    fsdp, depth = 2 * units[0].shape[0], units[0].shape[1]
    if depth % 8:
        units = assemble(place, units, [depth])
        depth = width
    double = units[0].shape[2]
    ff = double // 2
    d_cols = gy.shape[2]
    own = fsdp // 4

    def hidden_block(s, place_ref):
        return (place_ref[1] ^ (1 - s % 2)) * 2 + (place_ref[2] ^ (1 - s // 2))

    once = pl.Buffered(1)
    flops = 2 * rows * width * 4 * ff * 9
    return pl.pallas_call(
        feed_forward_kernel,
        grid_spec=pltpu.PrefetchScalarGridSpec(
            num_scalar_prefetch=1,
            grid=(4,),
            in_specs=[
                pl.BlockSpec((rows, width), lambda s, p: (0, 0), pipeline_mode=once),
                pl.BlockSpec((4, rows, d_cols), lambda s, p: (0, 0, 0), pipeline_mode=once),
                pl.BlockSpec((4, ff, d_cols), lambda s, p: (0, hidden_block(s, p), 0)),
            ]
            + [pl.BlockSpec(memory_space=pl.ANY)] * len(units),
            out_specs=[
                pl.BlockSpec((4, rows, d_cols), lambda s, p: (0, 0, 0), pipeline_mode=once),
                pl.BlockSpec((rows, width), lambda s, p: (0, 0), pipeline_mode=once),
                pl.BlockSpec((1, width, double), lambda s, p: (jnp.minimum(s, 1), 0, 0)),
                pl.BlockSpec((1, width, double), lambda s, p: (jnp.maximum(s - 2, 0), 0, 0)),
                pl.BlockSpec((2, own, od_rows, d_cols), lambda s, p: (0, hidden_block(s, p), 0, 0)),
                pl.BlockSpec((2, own, od_rows, d_cols), lambda s, p: (0, hidden_block(s, p), 0, 0)),
            ],
            scratch_shapes=[
                pltpu.VMEM((4, width // depth, depth, double), jnp.bfloat16),
                pltpu.VMEM((width, double), jnp.bfloat16),
                pltpu.VMEM((width, rows), jnp.bfloat16),
                pltpu.VMEM((rows, double), jnp.bfloat16),
                pltpu.VMEM((rows, ff), jnp.bfloat16),
                pltpu.SemaphoreType.DMA((4, fsdp)),
            ],
        ),
        out_shape=[
            jax.ShapeDtypeStruct((4, rows, d_cols), jnp.float32),
            jax.ShapeDtypeStruct((rows, width), jnp.float32),
            jax.ShapeDtypeStruct((2, width, double), jnp.bfloat16),
            jax.ShapeDtypeStruct((2, width, double), jnp.bfloat16),
            jax.ShapeDtypeStruct((2, fsdp, od_rows, d_cols), jnp.bfloat16),
            jax.ShapeDtypeStruct((2, fsdp, od_rows, d_cols), jnp.bfloat16),
        ],
        compiler_params=pltpu.CompilerParams(vmem_limit_bytes=60 << 20),
        cost_estimate=pl.CostEstimate(flops=flops, transcendentals=0, bytes_accessed=48 << 20),
        name="feed_forward",
    )(place, n2, gy, down, *units)


def after(value, *others):
    return lax.optimization_barrier((value, *others))[0]


def swap(value, axes):
    count = 2 ** len(axes)
    return lax.ppermute(value, axes, [(i, count - 1 - i) for i in range(count)])


def z_partner(value, mask, nz):
    return lax.ppermute(value, "z", [(i, i ^ mask) for i in range(nz)])


def gather_z(shard, nz, *before):
    if nz != 4:
        return lax.all_gather(shard, "z", axis=0, tiled=False)
    me = lax.axis_index("z")
    unit = jnp.zeros((nz,) + shard.shape, shard.dtype)
    pieces = [z_partner(shard, mask, nz) if mask else shard for mask in range(nz)]
    if before:
        pieces = lax.optimization_barrier((*pieces, *before))[:nz]
    for mask, piece in enumerate(pieces):
        unit = lax.dynamic_update_slice(unit, piece[None], (me ^ mask,) + (0,) * shard.ndim)
    return unit


def scatter_z(unit, nz):
    if nz != 4:
        return lax.psum_scatter(unit, "z", scatter_dimension=0, tiled=False).astype(jnp.float32)
    me = lax.axis_index("z")

    def part(mask):
        return lax.dynamic_index_in_dim(unit, me ^ mask, 0, keepdims=False)

    total = part(0).astype(jnp.float32)
    for mask in range(1, nz):
        total = total + z_partner(part(mask), mask, nz).astype(jnp.float32)
    return total


def units_of(own, along_y, along_x, along_both):
    four = (own, along_x, along_y, along_both)
    across = [swap(unit, ("c",)) for unit in four]
    order = []
    for yr in range(2):
        for xr in range(2):
            order += [four[yr * 2 + xr], across[yr * 2 + xr]]
    return order


def norm_back(values, scale_rows, gain_wide, upstream):
    weighted = gain_wide[None, :] * upstream
    return scale_rows * weighted - values * scale_rows**3 * jnp.mean(
        weighted * values, axis=1, keepdims=True
    )


def norm_scale(values):
    return lax.rsqrt(jnp.mean(values * values, axis=1, keepdims=True) + epsilon)


def shards(
    tokens,
    seq_lengths,
    norm1_gain,
    q_weight,
    k_weight,
    v_weight,
    o_weight,
    norm2_gain,
    gate_weight,
    up_weight,
    down_weight,
    cotangent,
):
    f32, bf16 = jnp.float32, jnp.bfloat16
    rows, width = tokens.shape
    nz = lax.axis_size("z")
    me_z, me_y, me_x, me_c = (lax.axis_index(a) for a in ("z", "y", "x", "c"))
    place = jnp.stack([me_y, me_x, me_c]).astype(jnp.int32)
    r_in, q_cols = q_weight.shape
    k_cols = k_weight.shape[1]
    qkv = q_cols + 2 * k_cols
    lanes = -(-(qkv + 2) // 128) * 128
    down_rows = down_weight.shape[0]
    o_rows = o_weight.shape[0]
    ff = gate_weight.shape[1]

    pack_a = jnp.concatenate(
        [
            q_weight,
            k_weight,
            v_weight,
            norm1_gain[:, None],
            norm2_gain[:, None],
            jnp.zeros((r_in, lanes - qkv - 2), bf16),
        ],
        axis=1,
    )
    filler = -(down_rows + o_rows) % 16
    pack_od = jnp.pad(jnp.concatenate([down_weight, o_weight], axis=0), ((0, filler), (0, 0)))
    pack_gu = jnp.concatenate([gate_weight, up_weight], axis=1)
    unit_a = gather_z(pack_a, nz)
    around = [swap(unit_a, axes) for axes in (("y",), ("x",), ("y", "x"))]
    units_a = units_of(unit_a, *around)
    [weights_a] = assemble(place, units_a, [r_in])
    unit_od = gather_z(after(pack_od, *units_a), nz)
    unit_gu = gather_z(after(pack_gu, unit_a), nz, *around)
    od_y, od_x = swap(unit_od, ("y",)), swap(unit_od, ("x",))
    gu_y, gu_x = swap(unit_gu, ("y",)), swap(unit_gu, ("x",))
    gain_one = weights_a[0, :, qkv].astype(f32)
    gain_two = weights_a[0, :, qkv + 1].astype(f32)

    lengths = seq_lengths[0]
    slots = jnp.arange(lengths.shape[0])
    ends = jnp.sum(jnp.where(slots[None, :] <= slots[:, None], lengths[None, :], 0), axis=1)
    places = jnp.arange(rows, dtype=jnp.int32)
    passed = (places[None, :] >= ends[:, None]).astype(jnp.int32)
    segment = jnp.sum(passed, axis=0)
    position = places - jnp.sum(passed * lengths[:, None], axis=0)
    live = (places < ends[-1]).astype(f32)
    same = jnp.arange(SEGMENT_ROWS)[:, None] == segment[None, :]
    onehot = same.astype(bf16)
    penalty = jnp.where(same, 0.0, masked_fill).astype(bf16)
    half = HEAD_SIZE // 2
    inverse = jnp.exp(
        -math.log(rope_base) * (jnp.arange(half, dtype=f32) * (2.0 / HEAD_SIZE))
    )
    angle = inverse[:, None] * position.astype(f32)[None, :]
    cos, sin = jnp.cos(angle), jnp.sin(angle)

    x = tokens.astype(f32)
    scale_one = norm_scale(x)
    n1 = (x * scale_one * gain_one[None, :]).astype(bf16)
    proj = lax.dot_general(
        weights_a, n1, (((1,), (1,)), ((), ())), preferred_element_type=f32
    )
    q_across = proj[:, :q_cols].reshape(QUERY_HEADS, 2, half, rows)
    k_across = proj[:, q_cols : q_cols + k_cols].reshape(KEY_VALUE_HEADS, 2, half, rows)
    v_across = proj[:, q_cols + k_cols : qkv].reshape(-1, rows).astype(bf16)

    def rope(u):
        u1, u2 = u[:, 0], u[:, 1]
        return (
            jnp.stack([u1 * cos - u2 * sin, u2 * cos + u1 * sin], axis=1)
            .astype(bf16)
            .reshape(-1, rows)
        )

    qr = rope(q_across) * jnp.asarray(1.0 / math.sqrt(HEAD_SIZE), bf16)
    kr = rope(k_across)
    qr = after(qr, unit_od, unit_gu)
    att, lse = attention_forward(onehot, penalty, qr, kr, v_across)
    od_y, od_x, gu_y, gu_x = (after(a, att) for a in (od_y, od_x, gu_y, gu_x))
    units_od = units_of(unit_od, od_y, od_x, swap(od_y, ("x",)))
    units_gu = units_of(unit_gu, gu_y, gu_x, swap(gu_x, ("y",)))
    down_all, o_all = assemble(place, units_od, [down_rows, o_rows + filler])
    o_all = o_all.reshape(4, 2 * nz, o_rows + filler, -1)[:, :, :o_rows].reshape(4, width, -1)
    o_full = jnp.concatenate([o_all[d] for d in range(4)], axis=1)
    hmid = x + contract(att, o_full, 0, 0)

    scale_two = norm_scale(hmid)
    n2 = (hmid * scale_two * gain_two[None, :]).astype(bf16)
    gy = live[:, None] * cotangent.astype(f32)
    d_cols = width // 4
    gy_low = gy.astype(bf16)
    gy_parts = jnp.stack([gy_low[:, d * d_cols : (d + 1) * d_cols] for d in range(4)])
    mixed_parts, dn2, gu_send, gu_keep, od_send, od_keep = feed_forward(
        place, n2, gy_parts, down_all, units_gu, down_rows + o_rows + filler
    )
    dh = gy + norm_back(hmid, scale_two, gain_two, dn2)
    da = dh.astype(bf16)

    def quarter(halves, k, y):
        part = lax.dynamic_slice(halves, (k, 0, y, 0, 0), (1, nz, 1) + halves.shape[3:])
        return part.reshape((nz,) + halves.shape[3:])

    gu_shape = (2, nz, 2, r_in, 2 * ff)
    gu_keep = gu_keep.reshape(gu_shape)
    gu_got = after(swap(gu_send, ("c",)), da).reshape(gu_shape)

    def both_gu(k, y):
        return quarter(gu_keep, k, y) + quarter(gu_got, k, y)

    gu_first = both_gu(0, 1 - me_y)
    gu_first_got = swap(gu_first, ("y",))

    da = after(da, gu_first)
    da_parts = jnp.stack([da[:, d * d_cols : (d + 1) * d_cols] for d in range(4)])
    grad_o = lax.dot_general(
        att, da_parts, (((1,), (1,)), ((), ())), preferred_element_type=f32
    )
    grad_o = grad_o.astype(bf16).transpose(1, 0, 2).reshape(2, 2, 2 * nz, o_rows, d_cols)
    datt = contract(o_full, da, 1, 1).astype(bf16)

    def with_o(parts, c):
        own = lax.dynamic_index_in_dim(grad_o, c, 1, keepdims=False)
        own = jnp.stack(
            [
                lax.dynamic_index_in_dim(own, 1 - me_x, 0, keepdims=False),
                lax.dynamic_index_in_dim(own, me_x, 0, keepdims=False),
            ]
        )
        return lax.dynamic_update_slice(parts, own, (0, 0, down_rows, 0))

    od_shape = (2, nz, 2, down_rows + o_rows + filler, d_cols)
    od_send = with_o(od_send, 1 - me_c)
    od_got = swap(od_send, ("c",)).reshape(od_shape)
    od_keep = with_o(od_keep, me_c).reshape(od_shape)

    def both_od(k, y):
        return quarter(od_keep, k, y) + quarter(od_got, k, y)

    od_first = both_od(0, 1 - me_y)
    od_first_got = swap(od_first, ("x",))

    back = functools.partial(attention_backward, onehot, penalty, cos, sin, qr, kr, v_across, att)
    first = back(after(datt, gu_first, od_first), lse, 0, 2)
    gu_x = both_gu(0, me_y) + after(gu_first_got, first[0])
    gu_second = both_gu(1, 1 - me_y)
    gu_x_got, gu_second_got = swap(gu_x, ("x",)), swap(gu_second, ("y",))
    second = back(after(datt, gu_x, gu_second, first[0]), lse, 2, 2)
    od_y = both_od(1, 1 - me_y) + after(od_first_got, second[0])
    od_second = both_od(0, me_y)
    od_y_got, od_second_got = swap(od_y, ("y",)), swap(od_second, ("x",))
    third = back(after(datt, od_y, od_second, second[0]), lse, 4, 1)
    dq, dk, dv = (jnp.concatenate(group) for group in zip(first, second, third))
    dproj = jnp.concatenate(
        [
            dq.reshape(4, q_cols, rows),
            dk.reshape(4, k_cols, rows),
            dv.reshape(4, k_cols, rows),
            jnp.zeros((4, lanes - qkv, rows), bf16),
        ],
        axis=1,
    )
    grad_a = lax.dot_general(dproj, n1, (((2,), (0,)), ((), ())), preferred_element_type=f32)
    grad_a = grad_a.transpose(0, 2, 1).astype(bf16).reshape(2, 2, nz, 2, r_in, lanes)
    a_send = lax.dynamic_index_in_dim(grad_a, 1 - me_c, 1, keepdims=False)
    a_keep = lax.dynamic_index_in_dim(grad_a, me_c, 1, keepdims=False)
    dn1 = lax.dot_general(
        after(dproj, a_send), weights_a, (((0, 1), (0, 2)), ((), ())), preferred_element_type=f32
    )
    grad_gain_two = jnp.sum(after(dn2, dn1) * hmid * scale_two, axis=0)
    gains = jnp.stack([jnp.sum(dn1 * x * scale_one, axis=0), grad_gain_two], axis=1)
    gains = (gains + swap(gains.astype(bf16), ("c",)).astype(f32)).astype(bf16)
    gains = jnp.pad(gains, ((0, 0), (qkv, lanes - qkv - 2)))
    gains = gains.reshape(1, nz, 2, r_in, lanes)
    a_sum = a_keep + swap(a_send, ("c",)) + gains
    def part_a(x, y):
        return lax.dynamic_index_in_dim(
            lax.dynamic_index_in_dim(a_sum, x, 0, keepdims=False), y, 1, keepdims=False
        )

    a_sends = [part_a(1 - me_x, me_y), part_a(me_x, 1 - me_y), part_a(1 - me_x, 1 - me_y)]
    a_got = [swap(part, axes) for part, axes in zip(a_sends, (("x",), ("y",), ("y", "x")))]
    gu_unit = both_gu(1, me_y) + after(gu_second_got, *a_sends) + after(gu_x_got, *a_sends)
    sum_gu = scatter_z(gu_unit, nz)
    od_unit = both_od(1, me_y) + after(od_second_got, gu_unit) + after(od_y_got, gu_unit)
    sum_od = scatter_z(od_unit, nz)
    a_got = [after(got, od_unit) for got in a_got]
    a_unit = part_a(me_x, me_y) + a_got[0] + a_got[1] + a_got[2]
    sum_a = scatter_z(a_unit, nz)
    mixed_late = after(mixed_parts, *a_sends, od_unit)
    mixed = (
        live[:, None] * (hmid + jnp.concatenate([mixed_late[d] for d in range(4)], axis=1))
    ).astype(bf16)
    grad_tokens = dh + norm_back(x, scale_one, gain_one, after(dn1, *a_sends, od_unit))
    return (
        mixed,
        grad_tokens,
        sum_a[:, qkv],
        sum_a[:, :q_cols],
        sum_a[:, q_cols : q_cols + k_cols],
        sum_a[:, q_cols + k_cols : qkv],
        sum_od[down_rows : down_rows + o_rows],
        sum_a[:, qkv + 1],
        sum_gu[:, :ff],
        sum_gu[:, ff:],
        sum_od[:down_rows],
    )


def solution(mesh):
    fsdp, dp = mesh.devices.shape
    assert dp == 4 and fsdp % 2 == 0
    split = Mesh(mesh.devices.reshape(fsdp // 2, 2, 2, 2), ("z", "y", "x", "c"))
    rows, grid, gain = P(("z", "y", "x", "c"), None), P(("z", "y"), ("x", "c")), P(("z", "y"))
    return jax.shard_map(
        shards,
        mesh=split,
        in_specs=(rows, rows, gain, grid, grid, grid, grid, gain, grid, grid, grid, rows),
        out_specs=(rows, rows, gain, grid, grid, grid, grid, gain, grid, grid, grid),
        check_vma=False,
    )
```
